768 devices in a mesh: section: 8 (over y), lat: 96 (over x, z, core).
Axes of the slice: x: 4, y: 8, z: 12, core: 2. Of those that a mesh axis runs over, the one named last changes fastest.
Arguments:
- grad_out: bfloat16 [8, 96, 180, 384], P('section', 'lat'), may hold values from -6 to 6
- spec_saved: bfloat16 [8, 96, 2, 27648], P('section', None, None, 'lat'), may hold values from -6 to 6
- w1: bfloat16 [8, 2, 96, 384], P('section'), may hold values from -0.4375 to 0.4375
- w2: bfloat16 [8, 2, 96, 384], P('section'), may hold values from -0.4375 to 0.4375
- b1: bfloat16 [8, 2, 384], P('section'), may hold values from -5 to 5
- mode_counts: int32 [96], replicated, may hold values from 1 to 72, as said below
- assignment: int32 [96], replicated, may hold values from 0 to 95, each once
Outputs:
- grad_input: bfloat16 [8, 96, 180, 384], P('section', 'lat')
- grad_w1: float32 [8, 2, 96, 384], P('section', None, None, 'lat')
- grad_w2: float32 [8, 2, 96, 384], P('section', None, None, 'lat')
- grad_b1: float32 [8, 2, 384], P('section', None, 'lat')
The draws below stay inside these ranges and needn't reach their ends.
Inputs may be any that keep to these rules, and one draw needn't show every extreme that they name: `mode_counts`: active modes shrink from the middle band toward both ends; the middle band keeps all 72. `assignment`: A permutation of the latitude bands.
All inputs are finite; a program needn't handle non-finite values.
Results may differ from the reference program's by a relative error of at most 0.018.
Values may be sent and summed in bfloat16 or wider, within the bound.
A program may use at most 64 MiB of HBM per device.

```python
import math
import jax
import jax.numpy as jnp
from jax import lax

NB = 4
BS = 96
KM = 72
LON = 180
D = 384
LAT_ROWS = 96
SECTIONS = 8


def draw_mode_counts(key, part):
    bands = jnp.arange(LAT_ROWS, dtype=jnp.int32)
    spread = jnp.abs(2 * bands - (LAT_ROWS - 1))
    base = KM - spread * KM // (2 * LAT_ROWS)
    jitter = jax.random.randint(key, (LAT_ROWS,), -(KM // 8), 1)
    counts = jnp.clip(base + jitter, 1, KM)
    counts = jnp.where(bands == LAT_ROWS // 2, KM, counts)
    return counts.astype(jnp.int32)


def shard_levels(own_key, dims, split, low, top_value):
    level = 1.0
    for position, blocks in split:
        draws = jax.random.uniform(jax.random.fold_in(jax.random.fold_in(own_key, 6), position), (blocks,), jnp.float32, low / len(split), top_value / len(split))
        level = level * jnp.repeat(jnp.exp(draws), dims[position] // blocks).reshape((-1,) + (1,) * (len(dims) - 1 - position))
    return level


def bell_draw(stream_key, shape, deviation, bound, split=(), kind=jnp.bfloat16):
    values = jax.random.normal(stream_key, shape, jnp.float32) * deviation
    if len(split) > 0:
        values = shard_levels(stream_key, shape, split, -0.22, 0.18) * values
    return jnp.clip(values, min=-bound, max=bound).astype(kind)


def setup_inputs(seed: int = 0) -> dict:
    splits = jax.random.split(jax.random.key(seed), 8)
    return {
        "grad_out": bell_draw(splits[0], (SECTIONS, LAT_ROWS, LON, D), 1.0, 6.0, ((0, 8), (1, 96))),
        "spec_saved": bell_draw(splits[1], (SECTIONS, LAT_ROWS, 2, KM * NB * BS), 1.0, 6.0, ((0, 8), (3, 96))),
        "w1": bell_draw(splits[2], (SECTIONS, 2, BS, D), (2 * BS) ** -0.5, 0.4375, ((0, 8),)),
        "w2": bell_draw(splits[3], (SECTIONS, 2, BS, D), (2 * BS) ** -0.5, 0.4375, ((0, 8),)),
        "b1": bell_draw(splits[4], (SECTIONS, 2, D), 1.0, 5.0, ((0, 8),)),
        "mode_counts": draw_mode_counts(jax.random.fold_in(splits[7], 71), 0),
        "assignment": jax.random.permutation(splits[6], LAT_ROWS).astype(jnp.int32),
    }


def lon_tables(n_modes, length):
    modes = jnp.arange(n_modes, dtype=jnp.int32)
    cells = jnp.arange(length, dtype=jnp.int32)
    phase = modes[:, None] * cells[None, :] % length
    angle = phase.astype(jnp.float32) * (2.0 * math.pi / length)
    factor = 1.0 / math.sqrt(length)
    cosine = jnp.cos(angle) * factor
    sine = jnp.sin(angle) * factor
    weight = jnp.where(modes == 0, 1.0, 2.0).astype(jnp.float32)[:, None]
    forward = jnp.stack([cosine, -sine]).astype(jnp.bfloat16)
    inverse = jnp.stack([cosine * weight, -sine * weight]).astype(jnp.bfloat16)
    return (forward, inverse)

def lat_table(latitude, n_rows):
    freqs = jnp.arange(n_rows, dtype=jnp.int32)
    phase = freqs[:, None] * latitude[None, :] % n_rows
    angle = phase.astype(jnp.float32) * (2.0 * math.pi / n_rows)
    factor = 1.0 / math.sqrt(n_rows)
    cosine = jnp.cos(angle) * factor
    sine = jnp.sin(angle) * factor
    upper = jnp.stack([cosine, sine], axis=-1)
    lower = jnp.stack([-sine, cosine], axis=-1)
    return jnp.stack([upper, lower], axis=1).astype(jnp.bfloat16)

def silu_slope(pre):
    sig = jax.nn.sigmoid(pre)
    return sig * (1.0 + pre * (1.0 - sig))

def apply_mat(vec, mat):
    return jnp.einsum('knmi,inj->knmj', vec, mat)

def adjoint_mat(vec, mat):
    return jnp.einsum('knmj,inj->knmi', vec, mat)

def outer_sum(left, right):
    return jnp.einsum('knmi,knmj->inj', left, right)

def section_grad(cotan, saved, w_first, w_second, bias, active, fwd_table, inv_table, table):
    f32 = jnp.float32
    bf16 = jnp.bfloat16
    cot = cotan.reshape(LAT_ROWS, LON, NB, BS).astype(f32)
    spec = jnp.einsum('cml,rlni->rcnmi', inv_table.astype(f32), cot)
    spec = (spec * active[:, None, None, :, None]).astype(bf16)
    grad_y = jnp.einsum('kerc,rcnmi->kenmi', table.astype(f32), spec.astype(f32)).astype(bf16)
    vin = saved.reshape(LAT_ROWS, 2, KM, NB, BS).astype(f32)
    vin = jnp.transpose(vin, (0, 1, 3, 2, 4))
    first = w_first.reshape(2, BS, NB, BS).astype(f32)
    second = w_second.reshape(2, BS, NB, BS).astype(f32)
    shift_b = bias.reshape(2, NB, BS).astype(f32)
    v_r = vin[:, 0]
    v_i = vin[:, 1]
    pre_r = apply_mat(v_r, first[0]) - apply_mat(v_i, first[1]) + shift_b[0][None, :, None, :]
    pre_i = apply_mat(v_i, first[0]) + apply_mat(v_r, first[1]) + shift_b[1][None, :, None, :]
    hid_r = jax.nn.silu(pre_r).astype(bf16).astype(f32)
    hid_i = jax.nn.silu(pre_i).astype(bf16).astype(f32)
    dy_r = grad_y[:, 0].astype(f32)
    dy_i = grad_y[:, 1].astype(f32)
    dh_r = adjoint_mat(dy_r, second[0]) + adjoint_mat(dy_i, second[1])
    dh_i = adjoint_mat(dy_i, second[0]) - adjoint_mat(dy_r, second[1])
    dp_r = (dh_r * silu_slope(pre_r)).astype(bf16).astype(f32)
    dp_i = (dh_i * silu_slope(pre_i)).astype(bf16).astype(f32)
    gw2 = jnp.stack([outer_sum(hid_r, dy_r) + outer_sum(hid_i, dy_i), outer_sum(hid_r, dy_i) - outer_sum(hid_i, dy_r)])
    gw1 = jnp.stack([outer_sum(v_r, dp_r) + outer_sum(v_i, dp_i), outer_sum(v_r, dp_i) - outer_sum(v_i, dp_r)])
    gb1 = jnp.stack([lax.optimization_barrier(jnp.sum(dp_r, axis=(0, 2))), lax.optimization_barrier(jnp.sum(dp_i, axis=(0, 2)))])
    dv_r = adjoint_mat(dp_r, first[0]) + adjoint_mat(dp_i, first[1])
    dv_i = adjoint_mat(dp_i, first[0]) - adjoint_mat(dp_r, first[1])
    grad_v = jnp.stack([dv_r, dv_i], axis=1).astype(bf16)
    band = jnp.einsum('kerc,kenmi->rcnmi', table.astype(f32), grad_v.astype(f32)).astype(bf16)
    band = band.astype(f32) * active[:, None, None, :, None]
    mixed = jnp.einsum('cml,rcnmi->rlni', fwd_table.astype(f32), band).astype(bf16)
    mixed = mixed.reshape(LAT_ROWS, LON, D)
    total = (cotan.astype(f32) + mixed.astype(f32)).astype(bf16)
    return (total, gw1.reshape(2, BS, D), gw2.reshape(2, BS, D), gb1.reshape(2, D))

def reference(grad_out, spec_saved, w1, w2, b1, mode_counts, assignment):
    fwd_table, inv_table = lon_tables(KM, LON)
    table = lat_table(assignment.astype(jnp.int32), LAT_ROWS)
    row_counts = mode_counts[assignment]
    active = (jnp.arange(KM, dtype=jnp.int32)[None, :] < row_counts[:, None]).astype(jnp.float32)

    def one_section(items):
        cotan, saved, w_first, w_second, bias = items
        return section_grad(cotan, saved, w_first, w_second, bias, active, fwd_table, inv_table, table)
    total, gw1, gw2, gb1 = lax.map(one_section, (grad_out, spec_saved, w1, w2, b1))
    zeros = jnp.zeros((1, LAT_ROWS, LON, D), dtype=jnp.bfloat16)
    grad_input = jnp.concatenate([total[1:], zeros], axis=0)
    return (grad_input, gw1, gw2, gb1)
```

```python
import functools
import math

import jax
import jax.numpy as jnp
import ml_dtypes
import numpy as np
from jax import lax
from jax.experimental import pallas as pl
from jax.experimental.pallas import tpu as pltpu
from jax.sharding import PartitionSpec as P

NB = 4
BS = 96
LANES = 128
SLOTS = 3
F32 = jnp.float32
BF16 = jnp.bfloat16
MESH = pl.DeviceIdType.MESH


def lon_consts(n_modes, length, half_z):
    modes = np.arange(n_modes)
    phase = (modes[:, None] * np.arange(length)[None, :]) % length
    angle = phase.astype(np.float32) * np.float32(2.0 * math.pi / length)
    factor = np.float32(1.0 / math.sqrt(length))
    cosine = np.cos(angle) * factor
    sine = np.sin(angle) * factor
    weight = np.where(modes == 0, 1.0, 2.0).astype(np.float32)[:, None]
    forward = np.stack([cosine, -sine])
    inverse = forward * weight
    q, zh, x, c = np.meshgrid(
        np.arange(SLOTS), np.arange(half_z), np.arange(NB), np.arange(2), indexing="ij"
    )
    m = (SLOTS * (x * half_z + zh) + q).reshape(-1)
    c = c.reshape(-1)
    inv = inverse[c, m].astype(ml_dtypes.bfloat16)
    fwd = np.ascontiguousarray(forward[c, m].T).astype(ml_dtypes.bfloat16)
    return inv, fwd, m.astype(np.float32)


def lat_consts(rows, n_z):
    freqs = np.arange(rows)
    phase = (freqs[:, None] * freqs[None, :]) % rows
    angle = phase.astype(np.float32) * np.float32(2.0 * math.pi / rows)
    factor = np.float32(1.0 / math.sqrt(rows))
    cosine = np.cos(angle) * factor
    sine = np.sin(angle) * factor
    top = np.stack([cosine, sine], axis=-1).reshape(rows, 2 * rows)
    low = np.stack([-sine, cosine], axis=-1).reshape(rows, 2 * rows)
    dft = np.concatenate([top, low], axis=0).astype(ml_dtypes.bfloat16)
    pick = np.zeros((NB, 2, n_z, 2, rows), np.float32)
    for x in range(NB):
        for core in range(2):
            for z in range(n_z):
                pick[x, core, z, :, (x * n_z + z) * 2 + core] = 2.0
    pick = pick.reshape(2 * rows, rows).astype(ml_dtypes.bfloat16)
    split = np.zeros((2, rows, rows, 2), np.float32)
    for part in range(2):
        split[part, np.arange(rows), np.arange(rows), part] = 1.0
    split = split.reshape(2 * rows, 2 * rows).astype(ml_dtypes.bfloat16)
    return dft, pick, split


def dot(a, b):
    return jnp.dot(a, b, preferred_element_type=F32)


def dot_nt(a, b):
    return lax.dot_general(a, b, (((1,), (1,)), ((), ())), preferred_element_type=F32)


def dot_tn(a, b):
    return lax.dot_general(a, b, (((0,), (0,)), ((), ())), preferred_element_type=F32)


def kernel(
    n_sec, n_z,
    counts, assign_s, assign_h, go_h, sv_h, w1_h, w2_h, b1_h,
    inv_h, fwd_h, mrow_h, mcol_h, dft_h, pick_h, split_h,
    out_gi, out_w1, out_w2, out_b1,
    assign, go, sv, w1, w2, b1, inv, fwd, mrow, mcol, dft, pick, split,
    send1, relay1, pencil, send2, relay2, band, gonext,
    quad1, quad2, vcat, hid, slope, dyc, dpc, tab, tab2,
    wsend, wrecv, zsend, zrecv,
    ld, lsem, s1, r1, s2, r2, sg, rg, s3, r3, s4, r4, sw, rw, sz, rz,
):
    rows = 8 * n_z
    half_z = n_z // 2
    jc = BS // (2 * n_z)
    sec = lax.axis_index("section")
    p = lax.axis_index("lat")
    x = p // (2 * n_z)
    z = lax.rem(p // 2, n_z)
    core = lax.rem(p, 2)
    q0 = 2 * x + core

    def at_z(zz):
        return x * (2 * n_z) + zz * 2 + core

    def at_q(q):
        return (q // 2) * (2 * n_z) + z * 2 + lax.rem(q, 2)

    def block_of(slot):
        return lax.rem(SLOTS * p + slot, NB)

    loads = []
    for i, (src, dst) in enumerate([
        (go_h, go), (inv_h, inv), (mrow_h, mrow), (w1_h, w1), (b1_h, b1), (w2_h, w2),
        (sv_h, sv), (split_h, split), (assign_h, assign), (pick_h, pick), (dft_h, dft),
        (fwd_h, fwd), (mcol_h, mcol),
    ]):
        copy = pltpu.make_async_copy(src, dst, ld.at[i])
        copy.start()
        loads.append(copy)

    barrier = pltpu.get_barrier_semaphore()

    def greet_z(i, carry):
        pl.semaphore_signal(barrier, inc=1, device_id=(sec, at_z(lax.rem(z + i, n_z))), device_id_type=MESH)
        return carry

    def greet_q(i, carry):
        pl.semaphore_signal(barrier, inc=1, device_id=(sec, at_q(lax.rem(q0 + i, 8))), device_id_type=MESH)
        return carry

    lax.fori_loop(1, n_z, greet_z, 0)
    lax.fori_loop(1, 8, greet_q, 0)

    @pl.when(sec < n_sec - 1)
    def _():
        pl.semaphore_signal(barrier, inc=1, device_id=(sec + 1, p), device_id_type=MESH)

    count = counts[assign_s[p]].astype(F32)
    for i in range(3):
        loads[i].wait()
    table = jnp.where(mrow[...] < count, inv[...], jnp.zeros_like(inv[...]))
    modes = dot(table, go[...])
    per_q = 8 * half_z
    lane_pad = jnp.zeros((per_q, LANES - BS), F32)
    for t in range(4):
        for j in range(SLOTS):
            q, n = divmod(SLOTS * t + j, NB)
            part = modes[q * per_q:(q + 1) * per_q, n * BS:(n + 1) * BS]
            part = jnp.concatenate([part, lane_pad], axis=1).astype(BF16)
            send1[:, t // 2, :, t % 2, j] = part.reshape(half_z, NB, 2, LANES)

    @pl.when(sec > 0)
    def _():
        pl.semaphore_wait(barrier, n_z + 7)

    @pl.when(sec == 0)
    def _():
        pl.semaphore_wait(barrier, n_z + 6)

    def send_z1(i, carry):
        d = jnp.where(lax.rem(i, 2) == 0, n_z // 2 + (i + 1) // 2, n_z // 2 - (i + 1) // 2)
        zz = lax.rem(z + d, n_z)
        pltpu.make_async_remote_copy(
            send1.at[zz // 2, lax.rem(zz, 2)], relay1.at[z], s1, r1.at[z],
            device_id=(sec, at_z(zz)), device_id_type=MESH,
        ).start()
        return carry

    lax.fori_loop(0, n_z - 1, send_z1, 0)
    own1 = pltpu.make_async_copy(send1.at[z // 2, lax.rem(z, 2)], relay1.at[z], lsem.at[0])
    own1.start()

    @pl.when(sec > 0)
    def _():
        pltpu.make_async_remote_copy(
            go, gonext, sg, rg, device_id=(sec - 1, p), device_id_type=MESH
        ).start()

    for i in range(3, 13):
        loads[i].wait()
    row_id = lax.broadcasted_iota(jnp.int32, (LANES, LANES), 0)
    bias = b1[...].astype(F32)

    def padded(mat, n):
        mat = mat[:, n * BS:(n + 1) * BS].astype(F32)
        mat = jnp.concatenate([mat, jnp.zeros((BS, LANES - BS), F32)], axis=1)
        return jnp.concatenate([mat, jnp.zeros((LANES - BS, LANES), F32)], axis=0)

    for n in range(NB):
        for which, (src, dst) in enumerate(((w1, quad1), (w2, quad2))):
            real, imag = padded(src[0], n), padded(src[1], n)
            top_r, top_i = real, imag
            if which == 0:
                shift = [
                    jnp.concatenate([bias[c:c + 1, n * BS:(n + 1) * BS], jnp.zeros((1, LANES - BS), F32)], axis=1)
                    for c in range(2)
                ]
                top_r = jnp.where(row_id == BS, shift[0], real)
                top_i = jnp.where(row_id == BS, shift[1], imag)
            dst[n, 0:LANES, 0:LANES] = top_r.astype(BF16)
            dst[n, 0:LANES, LANES:] = top_i.astype(BF16)
            dst[n, LANES:, 0:LANES] = (-imag).astype(BF16)
            dst[n, LANES:, LANES:] = real.astype(BF16)

    saved = dot(split[...], sv[...].reshape(2 * rows, SLOTS * BS))
    first_lane = lax.broadcasted_iota(jnp.int32, (rows, LANES - BS), 1) == 0
    one = jnp.where(first_lane, 1.0, 0.0).astype(F32)
    none = jnp.zeros((rows, LANES - BS), F32)
    for j in range(SLOTS):
        v = jnp.concatenate(
            [saved[0:rows, j * BS:(j + 1) * BS], one, saved[rows:, j * BS:(j + 1) * BS], none], axis=1
        ).astype(BF16)
        vcat[j] = v
        pre = dot(v, quad1[block_of(j)])
        sig = jax.nn.sigmoid(pre)
        hid[j] = (pre * sig).astype(BF16)
        slope[j] = sig * (1.0 + pre * (1.0 - sig))

    bands = jnp.broadcast_to(assign[...].astype(F32), (8, rows)).astype(BF16)
    target = dot_nt(pick[...], bands)[:, 0:1]
    row_part = lax.rem(lax.broadcasted_iota(jnp.int32, (2 * rows, 1), 0), 2).astype(F32)
    column = lax.broadcasted_iota(jnp.int32, (2 * rows, 2 * rows), 1).astype(F32)
    chosen = jnp.where(column == target + row_part, 1.0, 0.0).astype(BF16)
    tab[...] = dot_nt(dft[...], chosen).astype(BF16)
    tab2[...] = dot_nt(chosen, dft[...]).astype(BF16)

    own1.wait()

    def got_z1(i, carry):
        zz = lax.rem(z + i, n_z)
        pltpu.make_async_copy(relay1.at[zz], relay1.at[zz], r1.at[zz]).wait()
        return carry

    lax.fori_loop(1, n_z, got_z1, 0)

    def send_q1(i, carry):
        q = lax.rem(q0 + i, 8)
        pltpu.make_async_remote_copy(
            relay1.at[:, q // 2, lax.rem(q, 2)], pencil.at[q0], s2, r2,
            device_id=(sec, at_q(q)), device_id_type=MESH,
        ).start()
        return carry

    lax.fori_loop(1, 8, send_q1, 0)
    own2 = pltpu.make_async_copy(relay1.at[:, x, core], pencil.at[q0], lsem.at[1])
    own2.start()
    own2.wait()
    pltpu.make_async_copy(pencil.at[pl.ds(0, 7)], pencil.at[pl.ds(0, 7)], r2).wait()

    spec = jnp.concatenate([pencil[:, :, j].reshape(2 * rows, LANES) for j in range(SLOTS)], axis=1)
    grad_y = dot(tab[...], spec).astype(BF16)
    inner = []
    for j in range(SLOTS):
        lanes = slice(j * LANES, (j + 1) * LANES)
        dy = jnp.concatenate([grad_y[0:rows, lanes], grad_y[rows:, lanes]], axis=1)
        dyc[j] = dy
        n = block_of(j)
        dp = (dot_nt(dy, quad2[n]) * slope[j]).astype(BF16)
        dpc[j] = dp
        dv = dot_nt(dp, quad1[n]).astype(BF16)
        inner.append(jnp.concatenate([dv[:, 0:LANES], dv[:, LANES:]], axis=0))
    grad_u = dot(tab2[...], jnp.concatenate(inner, axis=1)).astype(BF16)
    for j in range(SLOTS):
        send2[:, :, j] = grad_u[:, j * LANES:(j + 1) * LANES].reshape(8, n_z, 2, LANES)

    def send_q2(i, carry):
        q = lax.rem(q0 + i, 8)
        pltpu.make_async_remote_copy(
            send2.at[q], relay2.at[x, core], s3, r3,
            device_id=(sec, at_q(q)), device_id_type=MESH,
        ).start()
        return carry

    lax.fori_loop(1, 8, send_q2, 0)
    own3 = pltpu.make_async_copy(send2.at[q0], relay2.at[x, core], lsem.at[2])
    own3.start()

    for j in range(SLOTS):
        for w, (left, right) in enumerate(((dpc, vcat), (dyc, hid))):
            prod = dot_tn(left[j], right[j])
            real = prod[0:BS, 0:LANES] + prod[LANES:LANES + BS, LANES:]
            imag = prod[LANES:LANES + BS, 0:LANES] - prod[0:BS, LANES:]
            for c, val in enumerate((real, imag)):
                val = val.astype(BF16).reshape(n_z, 2, jc, LANES)
                wsend[j, 0, 2 * w + c] = val[:, 0]
                wsend[j, 1, 2 * w + c] = val[:, 1]
    for j in range(SLOTS):
        n = block_of(j)
        for c in range(2):
            mine = jnp.logical_and(n == x, core == c)

            @pl.when(jnp.logical_not(mine))
            def _():
                pltpu.make_async_remote_copy(
                    wsend.at[j, c], wrecv.at[q0], sw.at[2 * j + c], rw.at[q0],
                    device_id=(sec, n * (2 * n_z) + z * 2 + c), device_id_type=MESH,
                ).start()

            @pl.when(mine)
            def _():
                pltpu.make_async_copy(wsend.at[j, c], wrecv.at[q0], rw.at[q0]).start()

    own3.wait()
    pltpu.make_async_copy(send2.at[pl.ds(0, 7)], send2.at[pl.ds(0, 7)], r3).wait()

    @pl.when(sec > 0)
    def _():
        def send_z2(i, carry):
            d = jnp.where(lax.rem(i, 2) == 0, n_z // 2 + (i + 1) // 2, n_z // 2 - (i + 1) // 2)
            zz = lax.rem(z + d + n_z, n_z)
            pltpu.make_async_remote_copy(
                relay2.at[:, :, zz], band.at[z // 2, lax.rem(z, 2)], s4, r4,
                device_id=(sec - 1, at_z(zz)), device_id_type=MESH,
            ).start()
            return carry

        lax.fori_loop(0, n_z, send_z2, 0)

    def has_block(src_core):
        return x != NB - 1 - (2 * lax.rem(z, 2) + src_core)

    zsum = jnp.zeros((4, n_z, jc, LANES), F32)
    for c in range(2):
        def gather(i, acc):
            q = 2 * i + c
            pltpu.make_async_copy(wrecv.at[q], wrecv.at[q], rw.at[q]).wait()
            return acc + wrecv[q].astype(F32)

        zsum = lax.cond(has_block(c), lambda acc: lax.fori_loop(0, NB, gather, acc), lambda acc: acc, zsum)
    zsum = zsum.astype(BF16)
    for w in range(4):
        zsend[:, w] = zsum[w]

    def send_zw(i, carry):
        zz = lax.rem(z + i, n_z)
        pltpu.make_async_remote_copy(
            zsend.at[zz], zrecv.at[z], sz, rz,
            device_id=(sec, at_z(zz)), device_id_type=MESH,
        ).start()
        return carry

    lax.fori_loop(1, n_z, send_zw, 0)
    own4 = pltpu.make_async_copy(zsend.at[z], zrecv.at[z], lsem.at[3])
    own4.start()

    @pl.when(sec < n_sec - 1)
    def _():
        pltpu.make_async_copy(band, band, r4).wait()
        pltpu.make_async_copy(gonext, gonext, rg).wait()
        blocks = []
        for n in range(NB):
            pieces = []
            for q in range(SLOTS):
                t, j = divmod(NB * q + n, SLOTS)
                pieces.append(band[:, t // 2, :, t % 2, j].reshape(per_q, LANES))
            blocks.append(jnp.concatenate(pieces, axis=0))
        table = jnp.where(mcol[...] < count, fwd[...], jnp.zeros_like(fwd[...]))
        mixed = dot(table, jnp.concatenate(blocks, axis=1))
        mixed = jnp.concatenate([mixed[:, n * LANES:n * LANES + BS] for n in range(NB)], axis=1)
        mixed = mixed.astype(BF16).astype(F32)
        out_gi[...] = (gonext[...].astype(F32) + mixed).astype(BF16)

    @pl.when(sec == n_sec - 1)
    def _():
        out_gi[...] = jnp.zeros_like(out_gi)

    own4.wait()
    pltpu.make_async_copy(zrecv.at[pl.ds(0, n_z - 1)], zrecv.at[pl.ds(0, n_z - 1)], rz).wait()
    total = jnp.sum(zrecv[...].astype(F32), axis=0).reshape(4 * jc, LANES)
    total = jnp.transpose(
        jnp.concatenate([total, jnp.zeros((LANES - 4 * jc, LANES), F32)], axis=0)
    )
    for c in range(2):
        out_w1[c] = total[0:BS, c * jc:(c + 1) * jc]
        out_w2[c] = total[0:BS, (2 + c) * jc:(3 + c) * jc]
        out_b1[c:c + 1, :] = total[BS:BS + 1, c * jc:(c + 1) * jc]

    pltpu.make_async_copy(relay1.at[pl.ds(0, n_z - 1)], relay1.at[pl.ds(0, n_z - 1)], s1).wait()
    pltpu.make_async_copy(pencil.at[pl.ds(0, 7)], pencil.at[pl.ds(0, 7)], s2).wait()
    pltpu.make_async_copy(send2.at[pl.ds(0, 7)], send2.at[pl.ds(0, 7)], s3).wait()
    pltpu.make_async_copy(zrecv.at[pl.ds(0, n_z - 1)], zrecv.at[pl.ds(0, n_z - 1)], sz).wait()

    @pl.when(sec > 0)
    def _():
        pltpu.make_async_copy(band, band, s4).wait()
        pltpu.make_async_copy(gonext, gonext, sg).wait()

    for j in range(SLOTS):
        for c in range(2):
            mine = jnp.logical_and(block_of(j) == x, core == c)

            @pl.when(jnp.logical_not(mine))
            def _():
                pltpu.make_async_copy(wsend.at[j, c], wsend.at[j, c], sw.at[2 * j + c]).wait()


def per_device(n_sec, n_lat, grad_out, spec_saved, w1, w2, b1, mode_counts, assignment):
    n_z = n_lat // 8
    half_z = n_z // 2
    rows = n_lat
    jc = BS // (2 * n_z)
    length, width = grad_out.shape[2:]
    n_modes = SLOTS * n_lat // NB
    inv, fwd, m = lon_consts(n_modes, length, half_z)
    dft, pick, split = lat_consts(rows, n_z)
    operands = [
        mode_counts, assignment, assignment.reshape(1, rows), grad_out.reshape(length, width),
        spec_saved.reshape(rows, 2, SLOTS * BS), w1.reshape(2, BS, width), w2.reshape(2, BS, width),
        b1.reshape(2, width), jnp.asarray(inv), jnp.asarray(fwd), jnp.asarray(m[:, None]),
        jnp.asarray(m[None, :]), jnp.asarray(dft), jnp.asarray(pick), jnp.asarray(split),
    ]
    vmem = pltpu.VMEM
    local = [vmem(operands[i].shape, operands[i].dtype) for i in (2, 3, 4, 5, 6, 7, 8, 9, 10, 11, 12, 13, 14)]
    tile = (SLOTS, 2, LANES)
    big = 2 * LANES
    scratch = local + [
        vmem((half_z, 2, NB, 2) + tile, BF16),
        vmem((n_z, NB, 2) + tile, BF16),
        vmem((8, n_z) + tile, BF16),
        vmem((8, n_z) + tile, BF16),
        vmem((NB, 2, n_z) + tile, BF16),
        vmem((half_z, 2, NB, 2) + tile, BF16),
        vmem((length, width), BF16),
        vmem((NB, big, big), BF16),
        vmem((NB, big, big), BF16),
        vmem((SLOTS, rows, big), BF16),
        vmem((SLOTS, rows, big), BF16),
        vmem((SLOTS, rows, big), F32),
        vmem((SLOTS, rows, big), BF16),
        vmem((SLOTS, rows, big), BF16),
        vmem((2 * rows, 2 * rows), BF16),
        vmem((2 * rows, 2 * rows), BF16),
        vmem((SLOTS, 2, 4, n_z, jc, LANES), BF16),
        vmem((8, 4, n_z, jc, LANES), BF16),
        vmem((n_z, 4, jc, LANES), BF16),
        vmem((n_z, 4, jc, LANES), BF16),
    ]
    dma = pltpu.SemaphoreType.DMA
    sems = [
        dma((13,)), dma((4,)), dma(()), dma((n_z,)), dma(()), dma(()), dma(()), dma(()),
        dma(()), dma(()), dma(()), dma(()), dma((6,)), dma((8,)), dma(()), dma(()),
    ]
    smem = pl.BlockSpec(memory_space=pltpu.SMEM)
    hbm = pl.BlockSpec(memory_space=pl.ANY)
    whole = pl.BlockSpec(memory_space=pltpu.VMEM)
    gi, gw1, gw2, gb1 = pl.pallas_call(
        functools.partial(kernel, n_sec, n_z),
        out_shape=(
            jax.ShapeDtypeStruct((length, width), BF16),
            jax.ShapeDtypeStruct((2, BS, jc), F32),
            jax.ShapeDtypeStruct((2, BS, jc), F32),
            jax.ShapeDtypeStruct((2, jc), F32),
        ),
        in_specs=[smem, smem] + [hbm] * 13,
        out_specs=(whole,) * 4,
        scratch_shapes=scratch + sems,
        compiler_params=pltpu.CompilerParams(collective_id=0, has_side_effects=True),
        name="filter_backward",
    )(*operands)
    return gi[None, None], gw1[None], gw2[None], gb1[None]


def solution(mesh):
    return jax.shard_map(
        functools.partial(per_device, mesh.shape["section"], mesh.shape["lat"]),
        mesh=mesh,
        in_specs=(
            P("section", "lat", None, None),
            P("section", None, None, "lat"),
            P("section", None, None, None),
            P("section", None, None, None),
            P("section", None, None),
            P(),
            P(),
        ),
        out_specs=(
            P("section", "lat", None, None),
            P("section", None, None, "lat"),
            P("section", None, None, "lat"),
            P("section", None, "lat"),
        ),
        check_vma=False,
    )
```

```python
import functools
import math

import jax
import jax.numpy as jnp
import ml_dtypes
import numpy as np
from jax import lax
from jax.experimental import pallas as pl
from jax.experimental.pallas import tpu as pltpu
from jax.sharding import PartitionSpec as P

NB = 4
BS = 96
LANES = 128
SLOTS = 3
F32 = jnp.float32
BF16 = jnp.bfloat16
MESH = pl.DeviceIdType.MESH


def lon_consts(n_modes, length, half_z):
    modes = np.arange(n_modes)
    phase = (modes[:, None] * np.arange(length)[None, :]) % length
    angle = phase.astype(np.float32) * np.float32(2.0 * math.pi / length)
    factor = np.float32(1.0 / math.sqrt(length))
    cosine = np.cos(angle) * factor
    sine = np.sin(angle) * factor
    weight = np.where(modes == 0, 1.0, 2.0).astype(np.float32)[:, None]
    forward = np.stack([cosine, -sine])
    inverse = forward * weight
    group = np.arange(NB * half_z).reshape(NB, half_z)
    out = []
    for table, order in ((inverse, group), (forward, group.T)):
        m = SLOTS * order.reshape(1, -1, 1) + np.arange(SLOTS).reshape(-1, 1, 1)
        m = np.broadcast_to(m, (SLOTS, NB * half_z, 2)).reshape(-1)
        c = np.arange(m.size) % 2
        out.append((table[c, m].astype(ml_dtypes.bfloat16), m.astype(np.float32)))
    (inv, m_inv), (fwd, m_fwd) = out
    return inv, m_inv[:, None], np.ascontiguousarray(fwd.T), m_fwd[None, :]


def lat_consts(rows, n_z):
    freqs = np.arange(rows)
    phase = (freqs[:, None] * freqs[None, :]) % rows
    angle = phase.astype(np.float32) * np.float32(2.0 * math.pi / rows)
    factor = np.float32(1.0 / math.sqrt(rows))
    cosine = np.cos(angle) * factor
    sine = np.sin(angle) * factor
    top = np.stack([cosine, sine], axis=-1).reshape(rows, 2 * rows)
    low = np.stack([-sine, cosine], axis=-1).reshape(rows, 2 * rows)
    dft = np.concatenate([top, low], axis=0).astype(ml_dtypes.bfloat16)
    pick = np.zeros((n_z, NB, 2, 2, rows), np.float32)
    for x in range(NB):
        for core in range(2):
            for z in range(n_z):
                pick[z, x, core, :, (x * n_z + z) * 2 + core] = 2.0
    pick = pick.reshape(2 * rows, rows).astype(ml_dtypes.bfloat16)
    split = np.zeros((2, rows, rows, 2), np.float32)
    for part in range(2):
        split[part, np.arange(rows), np.arange(rows), part] = 1.0
    split = split.reshape(2 * rows, 2 * rows).astype(ml_dtypes.bfloat16)
    return dft, pick, split


def dot(a, b):
    return jnp.dot(a, b, preferred_element_type=F32)


def dot_nt(a, b):
    return lax.dot_general(a, b, (((1,), (1,)), ((), ())), preferred_element_type=F32)


def dot_tn(a, b):
    return lax.dot_general(a, b, (((0,), (0,)), ((), ())), preferred_element_type=F32)


def kernel(
    n_sec, n_z,
    go_h, inv_h, minv_h, assign_h, counts_h, sv_h, split_h, w1_h, b1_h, w2_h, pick_h, dft_h, fwd_h, mfwd_h,
    out_gi, out_w1, out_w2, out_b1,
    go, inv, minv, assign, counts, sv, split, w1, b1, w2, pick, dft, fwd, mfwd,
    send1, relay1, pencil, send2, relay2, band, gonext,
    quad1, quad2, vsend, vrecv, vcat, hid, slope, tab, tab2,
    wsend, wrecv, zsend, zrecv,
    ld, s1, r1, s2, r2, sg, rg, s3, r3, s4, r4, sv_s, sv_r, sw, rw, sz, rz, tok_r, tok_l,
):
    rows = 8 * n_z
    half_z = n_z // 2
    jc = BS // (2 * n_z)
    sec = lax.axis_index("section")
    p = lax.axis_index("lat")
    x = p // (2 * n_z)
    z = lax.rem(p // 2, n_z)
    core = lax.rem(p, 2)
    odd = lax.rem(z, 2)
    block = 2 * odd + core
    line = 2 * x + core

    def at(xx, zz, cc):
        return xx * (2 * n_z) + zz * 2 + cc

    def signal(sem, section, device):
        pl.semaphore_signal(sem, inc=1, device_id=(section, device), device_id_type=MESH)

    def remote(src, dst, send, recv, section, device):
        return pltpu.make_async_remote_copy(
            src, dst, send, recv, device_id=(section, device), device_id_type=MESH
        )

    def wait_bytes(ref, sem):
        pltpu.make_async_copy(ref, ref, sem).wait()

    loads = []
    for i, (src, dst) in enumerate([
        (go_h, go), (inv_h, inv), (minv_h, minv), (assign_h, assign), (counts_h, counts), (sv_h, sv),
        (split_h, split), (w1_h, w1), (b1_h, b1), (w2_h, w2), (pick_h, pick), (dft_h, dft),
        (fwd_h, fwd), (mfwd_h, mfwd),
    ]):
        copy = pltpu.make_async_copy(src, dst, ld.at[i])
        copy.start()
        loads.append(copy)

    right, left = lax.rem(z + 1, n_z), lax.rem(z + n_z - 1, n_z)
    twin = z + 1 - 2 * odd
    others = [(2, 0), (2, 1), (1, 0), (1, 1), (3, 0), (3, 1), (0, 1)]
    barrier = pltpu.get_barrier_semaphore()
    signal(barrier, sec, at(x, right, core))
    signal(barrier, sec, at(x, left, core))
    signal(barrier, sec, at(x, twin, 1 - core))
    for dx, dc in others:
        signal(barrier, sec, at(lax.rem(x + dx, NB), z, lax.rem(core + dc, 2)))

    @pl.when(sec < n_sec - 1)
    def _():
        signal(barrier, sec + 1, p)

    for i in range(5):
        loads[i].wait()
    lane = lax.broadcasted_iota(jnp.int32, (1, rows), 1)
    own_band = jnp.sum(jnp.where(lane == p, assign[...], 0), axis=1, keepdims=True)
    count = jnp.sum(jnp.where(lane == own_band, counts[...], 0), axis=1, keepdims=True).astype(F32)
    table = jnp.where(minv[...] < count, inv[...].astype(F32), 0.0).astype(BF16)
    modes = dot(table, go[...])
    per_q = 8 * half_z
    lane_pad = jnp.zeros((per_q, LANES - BS), F32)
    for n in range(NB):
        for j in range(SLOTS):
            part = modes[j * per_q:(j + 1) * per_q, n * BS:(n + 1) * BS]
            part = jnp.concatenate([part, lane_pad], axis=1).astype(BF16)
            send1[:, n % 2, :, n // 2, j] = part.reshape(NB, half_z, 2, LANES)

    @pl.when(sec > 0)
    def _():
        pl.semaphore_wait(barrier, 11)

    @pl.when(sec == 0)
    def _():
        pl.semaphore_wait(barrier, 10)

    for dx, dc in others:
        xx, cc = lax.rem(x + dx, NB), lax.rem(core + dc, 2)
        remote(send1.at[xx, cc], relay1.at[line], s1, r1, sec, at(xx, z, cc)).start()
    pltpu.make_async_copy(send1.at[x, core], relay1.at[line], r1).start()
    if half_z > 1:
        signal(tok_r.at[2], sec, at(x, left, core))
        signal(tok_l.at[2], sec, at(x, right, core))

    loads[5].wait()
    loads[6].wait()
    saved = dot(split[...], sv[...].reshape(2 * rows, SLOTS * BS))
    first = jnp.logical_and(
        lax.broadcasted_iota(jnp.int32, (2 * rows, LANES - BS), 1) == 0,
        lax.broadcasted_iota(jnp.int32, (2 * rows, LANES - BS), 0) < rows,
    )
    one = jnp.where(first, 1.0, 0.0).astype(F32)
    for j in range(SLOTS):
        vsend[j] = jnp.concatenate([saved[:, j * BS:(j + 1) * BS], one], axis=1).astype(BF16)
    for j in range(SLOTS):
        q, n = (SLOTS * block + j) // NB, lax.rem(SLOTS * block + j, NB)

        @pl.when(n == block)
        def _():
            pltpu.make_async_copy(vsend.at[j], vrecv.at[q], sv_r.at[q]).start()

        @pl.when(n != block)
        def _():
            remote(
                vsend.at[j], vrecv.at[q], sv_s.at[j], sv_r.at[q], sec, at(x, z - odd + n // 2, lax.rem(n, 2))
            ).start()

    @pl.when(sec > 0)
    def _():
        remote(go, gonext, sg, rg, sec - 1, p).start()

    wait_bytes(relay1, r1)
    pltpu.make_async_copy(relay1.at[:, z // 2, odd], pencil.at[z], r2).start()
    for k in range(1, half_z + 1):
        if k > 1:
            pl.semaphore_wait(tok_r.at[k], 1)
            pl.semaphore_wait(tok_l.at[k], 1)
            if k < half_z:
                signal(tok_r.at[k + 1], sec, at(x, left, core))
                signal(tok_l.at[k + 1], sec, at(x, right, core))
        for d in (k, n_z - k)[:1 if 2 * k == n_z else 2]:
            zz = lax.rem(z + d, n_z)
            remote(relay1.at[:, zz // 2, lax.rem(zz, 2)], pencil.at[z], s2, r2, sec, at(x, zz, core)).start()

    for i in range(7, 14):
        loads[i].wait()
    row_id = lax.broadcasted_iota(jnp.int32, (LANES, LANES), 0)

    def padded(mat):
        mat = jnp.concatenate([mat.astype(F32), jnp.zeros((mat.shape[0], LANES - BS), F32)], axis=1)
        if mat.shape[0] == BS:
            mat = jnp.concatenate([mat, jnp.zeros((LANES - BS, LANES), F32)], axis=0)
        return mat

    for n in range(NB):
        lanes = slice(n * BS, (n + 1) * BS)

        @pl.when(block == n)
        def _():
            for src, dst in ((w1, quad1), (w2, quad2)):
                real, imag = padded(src[0, :, lanes]), padded(src[1, :, lanes])
                top_r, top_i = real, imag
                if src is w1:
                    bias = b1[...].astype(F32)
                    top_r = jnp.where(row_id == BS, padded(bias[0:1, lanes]), real)
                    top_i = jnp.where(row_id == BS, padded(bias[1:2, lanes]), imag)
                dst[0:LANES, 0:LANES] = top_r.astype(BF16)
                dst[0:LANES, LANES:] = top_i.astype(BF16)
                dst[LANES:, 0:LANES] = (-imag).astype(BF16)
                dst[LANES:, LANES:] = real.astype(BF16)

    bands = jnp.broadcast_to(assign[...].astype(F32), (8, rows)).astype(BF16)
    target = dot_nt(pick[...], bands)[:, 0:1]
    row_part = lax.rem(lax.broadcasted_iota(jnp.int32, (2 * rows, 1), 0), 2).astype(F32)
    column = lax.broadcasted_iota(jnp.int32, (2 * rows, 2 * rows), 1).astype(F32)
    chosen = jnp.where(column == target + row_part, 1.0, 0.0).astype(BF16)
    tab[...] = dot_nt(dft[...], chosen).astype(BF16)
    tab2[...] = dot_nt(chosen, dft[...]).astype(BF16)

    for q in range(SLOTS):
        wait_bytes(vrecv.at[q], sv_r.at[q])
        vcat[q * rows:(q + 1) * rows, 0:LANES] = vrecv[q, 0:rows]
        vcat[q * rows:(q + 1) * rows, LANES:] = vrecv[q, rows:]
    pre = dot(vcat[...], quad1[...])
    sig = jax.nn.sigmoid(pre)
    hid[...] = (pre * sig).astype(BF16)
    slope[...] = sig * (1.0 + pre * (1.0 - sig))

    wait_bytes(pencil, r2)

    spec = jnp.concatenate([pencil[:, :, j].reshape(2 * rows, LANES) for j in range(SLOTS)], axis=1)
    grad_y = dot(tab[...], spec).astype(BF16)
    dy = jnp.concatenate(
        [
            jnp.concatenate([grad_y[c * rows:(c + 1) * rows, j * LANES:(j + 1) * LANES] for c in range(2)], axis=1)
            for j in range(SLOTS)
        ],
        axis=0,
    )
    dp = (dot_nt(dy, quad2[...]) * slope[...]).astype(BF16)
    dv = dot_nt(dp, quad1[...]).astype(BF16)
    inner = jnp.concatenate(
        [
            jnp.concatenate([dv[j * rows:(j + 1) * rows, c * LANES:(c + 1) * LANES] for c in range(2)], axis=0)
            for j in range(SLOTS)
        ],
        axis=1,
    )
    grad_u = dot(tab2[...], inner).astype(BF16)
    for j in range(SLOTS):
        send2[:, :, j] = grad_u[:, j * LANES:(j + 1) * LANES].reshape(n_z, 8, 2, LANES)
    for dx, dc in others:
        xx, cc = lax.rem(x + dx, NB), lax.rem(core + dc, 2)
        remote(send2.at[:, 2 * xx + cc], relay2.at[x, core], s3, r3, sec, at(xx, z, cc)).start()
    pltpu.make_async_copy(send2.at[:, line], relay2.at[x, core], r3).start()

    for w, (lhs, rhs) in enumerate(((dp, vcat), (dy, hid))):
        prod = dot_tn(lhs, rhs[...])
        real = prod[0:BS, 0:LANES] + prod[LANES:LANES + BS, LANES:]
        imag = prod[LANES:LANES + BS, 0:LANES] - prod[0:BS, LANES:]
        for c, val in enumerate((real, imag)):
            val = val.astype(BF16).reshape(n_z, 2, jc, LANES)
            wsend[0, 2 * w + c] = val[:, 0]
            wsend[1, 2 * w + c] = val[:, 1]
    for c in range(2):
        mine = jnp.logical_and(block == x, core == c)

        @pl.when(jnp.logical_not(mine))
        def _():
            remote(wsend.at[c], wrecv.at[x], sw.at[c], rw.at[x], sec, at(block, z, c)).start()

        @pl.when(mine)
        def _():
            pltpu.make_async_copy(wsend.at[c], wrecv.at[x], rw.at[x]).start()

    wait_bytes(relay2, r3)

    @pl.when(sec > 0)
    def _():
        for i in range(n_z):
            d = (n_z + half_z + (i + 1) // 2 * (1 if i % 2 == 0 else -1)) % n_z
            zz = lax.rem(z + d, n_z)
            remote(
                relay2.at[:, :, zz], band.at[z // 2, odd], s4, r4, sec - 1, at(x, zz, core)
            ).start()

    summing = x // 2 == odd

    @pl.when(summing)
    def _():
        acc = None
        for i in range(NB):
            wait_bytes(wrecv.at[i], rw.at[i])
            part = wrecv[i].astype(F32)
            acc = part if acc is None else acc + part
        acc = acc.astype(BF16)
        for w in range(4):
            zsend[:, w] = acc[w]
        pltpu.make_async_copy(zsend.at[z], zrecv.at[z // 2], rz).start()
        for i in range(n_z - 1):
            d = (n_z + half_z + (i + 1) // 2 * (1 if i % 2 == 0 else -1)) % n_z
            zz = lax.rem(z + d, n_z)
            remote(zsend.at[zz], zrecv.at[z // 2], sz, rz, sec, at(x, zz, core)).start()

    @pl.when(sec < n_sec - 1)
    def _():
        wait_bytes(band, r4)
        wait_bytes(gonext, rg)
        blocks = []
        for n in range(NB):
            pieces = [band[:, n // 2, :, n % 2, j].reshape(per_q, LANES) for j in range(SLOTS)]
            blocks.append(jnp.concatenate(pieces, axis=0))
        table = jnp.where(mfwd[...] < count, fwd[...].astype(F32), 0.0).astype(BF16)
        mixed = dot(table, jnp.concatenate(blocks, axis=1))
        mixed = jnp.concatenate([mixed[:, n * LANES:n * LANES + BS] for n in range(NB)], axis=1)
        mixed = mixed.astype(BF16).astype(F32)
        out_gi[...] = (gonext[...].astype(F32) + mixed).astype(BF16)

    @pl.when(sec == n_sec - 1)
    def _():
        out_gi[...] = jnp.zeros_like(out_gi)

    wait_bytes(zrecv, rz)
    total = jnp.sum(zrecv[...].astype(F32), axis=0)
    out_w1[...] = total[0:2, :, 0:BS]
    out_w2[...] = total[2:4, :, 0:BS]
    flat = jnp.concatenate([total.reshape(4 * jc, LANES), jnp.zeros((LANES - 4 * jc, LANES), F32)], axis=0)
    flat = jnp.transpose(flat)
    for c in range(2):
        out_b1[c:c + 1, :] = flat[BS:BS + 1, c * jc:(c + 1) * jc]

    wait_bytes(relay1.at[pl.ds(0, 7)], s1)
    wait_bytes(pencil.at[pl.ds(0, n_z - 1)], s2)
    wait_bytes(relay1.at[pl.ds(0, 7)], s3)

    @pl.when(sec > 0)
    def _():
        wait_bytes(band, s4)
        wait_bytes(gonext, sg)

    @pl.when(summing)
    def _():
        wait_bytes(zsend.at[pl.ds(0, n_z - 1)], sz)

    for j in range(SLOTS):
        @pl.when(lax.rem(SLOTS * block + j, NB) != block)
        def _():
            wait_bytes(vsend.at[j], sv_s.at[j])

    for c in range(2):
        @pl.when(jnp.logical_not(jnp.logical_and(block == x, core == c)))
        def _():
            wait_bytes(wsend.at[c], sw.at[c])


def per_device(n_sec, n_lat, grad_out, spec_saved, w1, w2, b1, mode_counts, assignment):
    n_z = n_lat // 8
    half_z = n_z // 2
    rows = n_lat
    jc = BS // (2 * n_z)
    length, width = grad_out.shape[2:]
    n_modes = SLOTS * n_lat // NB
    inv, m_inv, fwd, m_fwd = lon_consts(n_modes, length, half_z)
    dft, pick, split = lat_consts(rows, n_z)
    operands = [
        grad_out.reshape(length, width), jnp.asarray(inv), jnp.asarray(m_inv), assignment.reshape(1, rows),
        mode_counts.reshape(1, rows), spec_saved.reshape(rows, 2, SLOTS * BS), jnp.asarray(split),
        w1.reshape(2, BS, width), b1.reshape(2, width), w2.reshape(2, BS, width), jnp.asarray(pick),
        jnp.asarray(dft), jnp.asarray(fwd), jnp.asarray(m_fwd),
    ]
    vmem = pltpu.VMEM
    tile = (SLOTS, 2, LANES)
    big = 2 * LANES
    scratch = [vmem(v.shape, v.dtype) for v in operands] + [
        vmem((NB, 2, half_z, 2) + tile, BF16),
        vmem((8, half_z, 2) + tile, BF16),
        vmem((n_z, 8) + tile, BF16),
        vmem((n_z, 8) + tile, BF16),
        vmem((NB, 2, n_z) + tile, BF16),
        vmem((half_z, 2, NB, 2) + tile, BF16),
        vmem((length, width), BF16),
        vmem((big, big), BF16),
        vmem((big, big), BF16),
        vmem((SLOTS, 2 * rows, LANES), BF16),
        vmem((SLOTS, 2 * rows, LANES), BF16),
        vmem((SLOTS * rows, big), BF16),
        vmem((SLOTS * rows, big), BF16),
        vmem((SLOTS * rows, big), F32),
        vmem((2 * rows, 2 * rows), BF16),
        vmem((2 * rows, 2 * rows), BF16),
        vmem((2, 4, n_z, jc, LANES), BF16),
        vmem((NB, 4, n_z, jc, LANES), BF16),
        vmem((n_z, 4, jc, LANES), BF16),
        vmem((half_z, 4, jc, LANES), BF16),
    ]
    dma = pltpu.SemaphoreType.DMA
    sems = [
        dma((14,)), dma(()), dma(()), dma(()), dma(()), dma(()), dma(()), dma(()), dma(()),
        dma(()), dma(()), dma((SLOTS,)), dma((SLOTS,)), dma((2,)), dma((NB,)), dma(()), dma(()),
        pltpu.SemaphoreType.REGULAR((half_z + 1,)), pltpu.SemaphoreType.REGULAR((half_z + 1,)),
    ]
    hbm = pl.BlockSpec(memory_space=pl.ANY)
    whole = pl.BlockSpec(memory_space=pltpu.VMEM)
    gi, gw1, gw2, gb1 = pl.pallas_call(
        functools.partial(kernel, n_sec, n_z),
        out_shape=(
            jax.ShapeDtypeStruct((length, width), BF16),
            jax.ShapeDtypeStruct((2, jc, BS), F32),
            jax.ShapeDtypeStruct((2, jc, BS), F32),
            jax.ShapeDtypeStruct((2, jc), F32),
        ),
        in_specs=[hbm] * 14,
        out_specs=(whole,) * 4,
        scratch_shapes=scratch + sems,
        compiler_params=pltpu.CompilerParams(collective_id=0, has_side_effects=True),
        name="filter_backward",
    )(*operands)
    return gi[None, None], jnp.swapaxes(gw1, 1, 2)[None], jnp.swapaxes(gw2, 1, 2)[None], gb1[None]


def solution(mesh):
    return jax.shard_map(
        functools.partial(per_device, mesh.shape["section"], mesh.shape["lat"]),
        mesh=mesh,
        in_specs=(
            P("section", "lat", None, None),
            P("section", None, None, "lat"),
            P("section", None, None, None),
            P("section", None, None, None),
            P("section", None, None),
            P(),
            P(),
        ),
        out_specs=(
            P("section", "lat", None, None),
            P("section", None, None, "lat"),
            P("section", None, None, "lat"),
            P("section", None, "lat"),
        ),
        check_vma=False,
    )
```

```python
import functools
import math

import jax
import jax.numpy as jnp
import ml_dtypes
import numpy as np
from jax import lax
from jax.experimental import pallas as pl
from jax.experimental.pallas import tpu as pltpu
from jax.sharding import PartitionSpec as P

NB = 4
BS = 96
LANES = 128
SLOTS = 3
F32 = jnp.float32
BF16 = jnp.bfloat16
MESH = pl.DeviceIdType.MESH


def lon_consts(n_modes, length, half_z):
    modes = np.arange(n_modes)
    phase = (modes[:, None] * np.arange(length)[None, :]) % length
    angle = phase.astype(np.float32) * np.float32(2.0 * math.pi / length)
    factor = np.float32(1.0 / math.sqrt(length))
    cosine = np.cos(angle) * factor
    sine = np.sin(angle) * factor
    weight = np.where(modes == 0, 1.0, 2.0).astype(np.float32)[:, None]
    forward = np.stack([cosine, -sine])
    inverse = forward * weight
    group = np.arange(NB * half_z).reshape(NB, half_z)
    out = []
    for table, order in ((inverse, group), (forward, group.T)):
        m = SLOTS * order.reshape(1, -1, 1) + np.arange(SLOTS).reshape(-1, 1, 1)
        m = np.broadcast_to(m, (SLOTS, NB * half_z, 2)).reshape(-1)
        c = np.arange(m.size) % 2
        out.append((table[c, m].astype(ml_dtypes.bfloat16), m.astype(np.float32)))
    (inv, m_inv), (fwd, m_fwd) = out
    return inv, m_inv[:, None], np.ascontiguousarray(fwd.T), m_fwd[None, :]


def lat_consts(rows, n_z):
    freqs = np.arange(rows)
    phase = (freqs[:, None] * freqs[None, :]) % rows
    angle = phase.astype(np.float32) * np.float32(2.0 * math.pi / rows)
    factor = np.float32(1.0 / math.sqrt(rows))
    cosine = np.cos(angle) * factor
    sine = np.sin(angle) * factor
    top = np.stack([cosine, sine], axis=-1).reshape(rows, 2 * rows)
    low = np.stack([-sine, cosine], axis=-1).reshape(rows, 2 * rows)
    dft = np.concatenate([top, low], axis=0).astype(ml_dtypes.bfloat16)
    pick = np.zeros((n_z, NB, 2, 2, rows), np.float32)
    for x in range(NB):
        for core in range(2):
            for z in range(n_z):
                pick[z, x, core, :, (x * n_z + z) * 2 + core] = 2.0
    pick = pick.reshape(2 * rows, rows).astype(ml_dtypes.bfloat16)
    split = np.zeros((2, rows, rows, 2), np.float32)
    for part in range(2):
        split[part, np.arange(rows), np.arange(rows), part] = 1.0
    split = split.reshape(2 * rows, 2 * rows).astype(ml_dtypes.bfloat16)
    return dft, pick, split


def dot(a, b):
    return jnp.dot(a, b, preferred_element_type=F32)


def dot_nt(a, b):
    return lax.dot_general(a, b, (((1,), (1,)), ((), ())), preferred_element_type=F32)


def dot_tn(a, b):
    return lax.dot_general(a, b, (((0,), (0,)), ((), ())), preferred_element_type=F32)


def kernel(
    n_sec, n_z,
    go_h, inv_h, minv_h, assign_h, counts_h, sv_h, split_h, w1_h, b1_h, w2_h, pick_h, dft_h, fwd_h, mfwd_h,
    out_gi, out_w1, out_w2, out_b1,
    go, inv, minv, assign, counts, sv, split, w1, b1, w2, pick, dft, fwd, mfwd,
    send1, pencil, send2, band, gonext,
    quad1, quad2, vsend, vrecv, vcat, hid, slope, tab, tab2,
    wsend, wrecv,
    ld, s1, r1, sg, rg, s4, r4, sv_s, sv_r, sw, rw,
):
    rows = 8 * n_z
    half_z = n_z // 2
    jc = BS // (2 * n_z)
    sec = lax.axis_index("section")
    p = lax.axis_index("lat")
    x = p // (2 * n_z)
    z = lax.rem(p // 2, n_z)
    core = lax.rem(p, 2)
    odd = lax.rem(z, 2)
    block = 2 * odd + core
    line = 2 * x + core

    def at(xx, zz, cc):
        return xx * (2 * n_z) + zz * 2 + cc

    def signal(sem, section, device):
        pl.semaphore_signal(sem, inc=1, device_id=(section, device), device_id_type=MESH)

    def remote(src, dst, send, recv, section, device):
        return pltpu.make_async_remote_copy(
            src, dst, send, recv, device_id=(section, device), device_id_type=MESH
        )

    def wait_bytes(ref, sem):
        pltpu.make_async_copy(ref, ref, sem).wait()

    def far_first(i):
        half = (i + 1) // 2
        return lax.rem(z + n_z + half_z + jnp.where(lax.rem(i, 2) == 0, half, -half), n_z)

    loads = []
    for i, (src, dst) in enumerate([
        (go_h, go), (inv_h, inv), (minv_h, minv), (assign_h, assign), (counts_h, counts), (sv_h, sv),
        (split_h, split), (w1_h, w1), (b1_h, b1), (w2_h, w2), (pick_h, pick), (dft_h, dft),
        (fwd_h, fwd), (mfwd_h, mfwd),
    ]):
        copy = pltpu.make_async_copy(src, dst, ld.at[i])
        copy.start()
        loads.append(copy)

    barrier = pltpu.get_barrier_semaphore()

    def greet(i, carry):
        signal(barrier, sec, lax.rem(p + i, rows))
        return carry

    lax.fori_loop(1, rows, greet, 0)

    @pl.when(sec < n_sec - 1)
    def _():
        signal(barrier, sec + 1, p)

    for i in range(5):
        loads[i].wait()
    lane = lax.broadcasted_iota(jnp.int32, (1, rows), 1)
    own_band = jnp.sum(jnp.where(lane == p, assign[...], 0), axis=1, keepdims=True)
    count = jnp.sum(jnp.where(lane == own_band, counts[...], 0), axis=1, keepdims=True).astype(F32)
    table = jnp.where(minv[...] < count, inv[...].astype(F32), 0.0).astype(BF16)
    modes = dot(table, go[...])
    per_q = 8 * half_z
    lane_pad = jnp.zeros((per_q, LANES - BS), F32)
    for n in range(NB):
        for j in range(SLOTS):
            part = modes[j * per_q:(j + 1) * per_q, n * BS:(n + 1) * BS]
            part = jnp.concatenate([part, lane_pad], axis=1).astype(BF16)
            send1[:, n % 2, :, n // 2, j] = part.reshape(NB, half_z, 2, LANES)

    pl.semaphore_wait(barrier, rows - 1 + (sec > 0).astype(jnp.int32))

    def spread(i, carry):
        zz = far_first(i)

        def one(k, inner):
            q = lax.rem(line + k + 3, 8)
            xx, cc = q // 2, lax.rem(q, 2)
            target = at(xx, zz, cc)

            @pl.when(target != p)
            def _():
                remote(
                    send1.at[xx, cc, zz // 2, lax.rem(zz, 2)], pencil.at[8 * z + line], s1, r1, sec, target
                ).start()

            return inner

        return lax.fori_loop(0, 8, one, carry)

    lax.fori_loop(0, n_z, spread, 0)
    pltpu.make_async_copy(send1.at[x, core, z // 2, odd], pencil.at[8 * z + line], r1).start()

    loads[5].wait()
    loads[6].wait()
    saved = dot(split[...], sv[...].reshape(2 * rows, SLOTS * BS))
    first = jnp.logical_and(
        lax.broadcasted_iota(jnp.int32, (2 * rows, LANES - BS), 1) == 0,
        lax.broadcasted_iota(jnp.int32, (2 * rows, LANES - BS), 0) < rows,
    )
    one = jnp.where(first, 1.0, 0.0).astype(F32)
    for j in range(SLOTS):
        vsend[j] = jnp.concatenate([saved[:, j * BS:(j + 1) * BS], one], axis=1).astype(BF16)
    for j in range(SLOTS):
        q, n = (SLOTS * block + j) // NB, lax.rem(SLOTS * block + j, NB)

        @pl.when(n == block)
        def _():
            pltpu.make_async_copy(vsend.at[j], vrecv.at[q], sv_r.at[q]).start()

        @pl.when(n != block)
        def _():
            remote(
                vsend.at[j], vrecv.at[q], sv_s.at[j], sv_r.at[q], sec, at(x, z - odd + n // 2, lax.rem(n, 2))
            ).start()

    @pl.when(sec > 0)
    def _():
        remote(go, gonext, sg, rg, sec - 1, p).start()

    for i in range(7, 14):
        loads[i].wait()
    row_id = lax.broadcasted_iota(jnp.int32, (LANES, LANES), 0)

    def padded(mat):
        mat = jnp.concatenate([mat.astype(F32), jnp.zeros((mat.shape[0], LANES - BS), F32)], axis=1)
        if mat.shape[0] == BS:
            mat = jnp.concatenate([mat, jnp.zeros((LANES - BS, LANES), F32)], axis=0)
        return mat

    for n in range(NB):
        lanes = slice(n * BS, (n + 1) * BS)

        @pl.when(block == n)
        def _():
            for src, dst in ((w1, quad1), (w2, quad2)):
                real, imag = padded(src[0, :, lanes]), padded(src[1, :, lanes])
                top_r, top_i = real, imag
                if src is w1:
                    bias = b1[...].astype(F32)
                    top_r = jnp.where(row_id == BS, padded(bias[0:1, lanes]), real)
                    top_i = jnp.where(row_id == BS, padded(bias[1:2, lanes]), imag)
                dst[0:LANES, 0:LANES] = top_r.astype(BF16)
                dst[0:LANES, LANES:] = top_i.astype(BF16)
                dst[LANES:, 0:LANES] = (-imag).astype(BF16)
                dst[LANES:, LANES:] = real.astype(BF16)

    bands = jnp.broadcast_to(assign[...].astype(F32), (8, rows)).astype(BF16)
    target = dot_nt(pick[...], bands)[:, 0:1]
    row_part = lax.rem(lax.broadcasted_iota(jnp.int32, (2 * rows, 1), 0), 2).astype(F32)
    column = lax.broadcasted_iota(jnp.int32, (2 * rows, 2 * rows), 1).astype(F32)
    chosen = jnp.where(column == target + row_part, 1.0, 0.0).astype(BF16)
    tab[...] = dot_nt(dft[...], chosen).astype(BF16)
    tab2[...] = dot_nt(chosen, dft[...]).astype(BF16)

    for q in range(SLOTS):
        wait_bytes(vrecv.at[q], sv_r.at[q])
        vcat[q * rows:(q + 1) * rows, 0:LANES] = vrecv[q, 0:rows]
        vcat[q * rows:(q + 1) * rows, LANES:] = vrecv[q, rows:]
    pre = dot(vcat[...], quad1[...])
    sig = jax.nn.sigmoid(pre)
    hid[...] = (pre * sig).astype(BF16)
    slope[...] = sig * (1.0 + pre * (1.0 - sig))

    wait_bytes(pencil, r1)

    spec = jnp.concatenate([pencil[:, j].reshape(2 * rows, LANES) for j in range(SLOTS)], axis=1)
    grad_y = dot(tab[...], spec).astype(BF16)
    dy = jnp.concatenate(
        [
            jnp.concatenate([grad_y[c * rows:(c + 1) * rows, j * LANES:(j + 1) * LANES] for c in range(2)], axis=1)
            for j in range(SLOTS)
        ],
        axis=0,
    )
    dp = (dot_nt(dy, quad2[...]) * slope[...]).astype(BF16)
    dv = dot_nt(dp, quad1[...]).astype(BF16)
    inner = jnp.concatenate(
        [
            jnp.concatenate([dv[j * rows:(j + 1) * rows, c * LANES:(c + 1) * LANES] for c in range(2)], axis=0)
            for j in range(SLOTS)
        ],
        axis=1,
    )
    grad_u = dot(tab2[...], inner).astype(BF16)
    for j in range(SLOTS):
        send2[:, j] = grad_u[:, j * LANES:(j + 1) * LANES].reshape(rows, 2, LANES)

    @pl.when(sec > 0)
    def _():
        def plane(i, carry):
            zz = far_first(i)

            def one(k, inner_carry):
                q = lax.rem(line + k + 3, 8)
                xx, cc = q // 2, lax.rem(q, 2)
                remote(
                    send2.at[8 * zz + q], band.at[z // 2, odd, x, core], s4, r4, sec - 1, at(xx, zz, cc)
                ).start()
                return inner_carry

            return lax.fori_loop(0, 8, one, carry)

        lax.fori_loop(0, n_z, plane, 0)

    for w, (lhs, rhs) in enumerate(((dp, vcat), (dy, hid))):
        prod = dot_tn(lhs, rhs[...])
        real = prod[0:BS, 0:LANES] + prod[LANES:LANES + BS, LANES:]
        imag = prod[LANES:LANES + BS, 0:LANES] - prod[0:BS, LANES:]
        for c, val in enumerate((real, imag)):
            wsend[:, 2 * w + c] = val.astype(BF16).reshape(2 * n_z, jc, LANES)
    home = at(block, 0, 0)
    share = x * half_z + z // 2

    def columns(i, carry):
        to = lax.rem(2 * z + core + n_z + i, 2 * n_z)

        @pl.when(home + to != p)
        def _():
            remote(wsend.at[to], wrecv.at[share], sw, rw, sec, home + to).start()

        return carry

    lax.fori_loop(0, 2 * n_z, columns, 0)

    @pl.when(x == block)
    def _():
        pltpu.make_async_copy(wsend.at[2 * z + core], wrecv.at[share], rw).start()

    @pl.when(sec < n_sec - 1)
    def _():
        wait_bytes(band, r4)
        wait_bytes(gonext, rg)
        blocks = []
        for n in range(NB):
            pieces = [band[:, n // 2, :, n % 2, j].reshape(per_q, LANES) for j in range(SLOTS)]
            blocks.append(jnp.concatenate(pieces, axis=0))
        table = jnp.where(mfwd[...] < count, fwd[...].astype(F32), 0.0).astype(BF16)
        mixed = dot(table, jnp.concatenate(blocks, axis=1))
        mixed = jnp.concatenate([mixed[:, n * LANES:n * LANES + BS] for n in range(NB)], axis=1)
        mixed = mixed.astype(BF16).astype(F32)
        out_gi[...] = (gonext[...].astype(F32) + mixed).astype(BF16)

    @pl.when(sec == n_sec - 1)
    def _():
        out_gi[...] = jnp.zeros_like(out_gi)

    wait_bytes(wrecv, rw)
    total = jnp.sum(wrecv[...].astype(F32), axis=0)
    out_w1[...] = total[0:2, :, 0:BS]
    out_w2[...] = total[2:4, :, 0:BS]
    flat = jnp.concatenate([total.reshape(4 * jc, LANES), jnp.zeros((LANES - 4 * jc, LANES), F32)], axis=0)
    flat = jnp.transpose(flat)
    for c in range(2):
        out_b1[c:c + 1, :] = flat[BS:BS + 1, c * jc:(c + 1) * jc]

    wait_bytes(pencil.at[pl.ds(0, rows - 1)], s1)

    @pl.when(sec > 0)
    def _():
        wait_bytes(band, s4)
        wait_bytes(gonext, sg)

    @pl.when(x == block)
    def _():
        wait_bytes(wsend.at[pl.ds(0, 2 * n_z - 1)], sw)

    @pl.when(x != block)
    def _():
        wait_bytes(wsend, sw)

    for j in range(SLOTS):
        @pl.when(lax.rem(SLOTS * block + j, NB) != block)
        def _():
            wait_bytes(vsend.at[j], sv_s.at[j])


def per_device(n_sec, n_lat, grad_out, spec_saved, w1, w2, b1, mode_counts, assignment):
    n_z = n_lat // 8
    half_z = n_z // 2
    rows = n_lat
    jc = BS // (2 * n_z)
    length, width = grad_out.shape[2:]
    n_modes = SLOTS * n_lat // NB
    inv, m_inv, fwd, m_fwd = lon_consts(n_modes, length, half_z)
    dft, pick, split = lat_consts(rows, n_z)
    operands = [
        grad_out.reshape(length, width), jnp.asarray(inv), jnp.asarray(m_inv), assignment.reshape(1, rows),
        mode_counts.reshape(1, rows), spec_saved.reshape(rows, 2, SLOTS * BS), jnp.asarray(split),
        w1.reshape(2, BS, width), b1.reshape(2, width), w2.reshape(2, BS, width), jnp.asarray(pick),
        jnp.asarray(dft), jnp.asarray(fwd), jnp.asarray(m_fwd),
    ]
    vmem = pltpu.VMEM
    tile = (SLOTS, 2, LANES)
    big = 2 * LANES
    scratch = [vmem(v.shape, v.dtype) for v in operands] + [
        vmem((NB, 2, half_z, 2) + tile, BF16),
        vmem((rows,) + tile, BF16),
        vmem((rows,) + tile, BF16),
        vmem((half_z, 2, NB, 2) + tile, BF16),
        vmem((length, width), BF16),
        vmem((big, big), BF16),
        vmem((big, big), BF16),
        vmem((SLOTS, 2 * rows, LANES), BF16),
        vmem((SLOTS, 2 * rows, LANES), BF16),
        vmem((SLOTS * rows, big), BF16),
        vmem((SLOTS * rows, big), BF16),
        vmem((SLOTS * rows, big), F32),
        vmem((2 * rows, 2 * rows), BF16),
        vmem((2 * rows, 2 * rows), BF16),
        vmem((2 * n_z, 4, jc, LANES), BF16),
        vmem((NB * half_z, 4, jc, LANES), BF16),
    ]
    dma = pltpu.SemaphoreType.DMA
    sems = [
        dma((14,)), dma(()), dma(()), dma(()), dma(()), dma(()), dma(()), dma((SLOTS,)), dma((SLOTS,)),
        dma(()), dma(()),
    ]
    hbm = pl.BlockSpec(memory_space=pl.ANY)
    whole = pl.BlockSpec(memory_space=pltpu.VMEM)
    gi, gw1, gw2, gb1 = pl.pallas_call(
        functools.partial(kernel, n_sec, n_z),
        out_shape=(
            vmem((length, width), BF16),
            vmem((2, jc, BS), F32),
            vmem((2, jc, BS), F32),
            vmem((2, jc), F32),
        ),
        in_specs=[hbm] * 14,
        out_specs=(whole,) * 4,
        scratch_shapes=scratch + sems,
        compiler_params=pltpu.CompilerParams(collective_id=0, has_side_effects=True),
        name="filter_backward",
    )(*operands)
    return gi[None, None], jnp.swapaxes(gw1, 1, 2)[None], jnp.swapaxes(gw2, 1, 2)[None], gb1[None]


def solution(mesh):
    return jax.shard_map(
        functools.partial(per_device, mesh.shape["section"], mesh.shape["lat"]),
        mesh=mesh,
        in_specs=(
            P("section", "lat", None, None),
            P("section", None, None, "lat"),
            P("section", None, None, None),
            P("section", None, None, None),
            P("section", None, None),
            P(),
            P(),
        ),
        out_specs=(
            P("section", "lat", None, None),
            P("section", None, None, "lat"),
            P("section", None, None, "lat"),
            P("section", None, "lat"),
        ),
        check_vma=False,
    )
```

```python
import functools
import math

import jax
import jax.numpy as jnp
import ml_dtypes
import numpy as np
from jax import lax
from jax.experimental import pallas as pl
from jax.experimental.pallas import tpu as pltpu
from jax.sharding import PartitionSpec as P

NB = 4
BS = 96
LANES = 128
SLOTS = 3
F32 = jnp.float32
BF16 = jnp.bfloat16
MESH = pl.DeviceIdType.MESH


def lon_consts(n_modes, length, half_z):
    modes = np.arange(n_modes)
    phase = (modes[:, None] * np.arange(length)[None, :]) % length
    angle = phase.astype(np.float32) * np.float32(2.0 * math.pi / length)
    factor = np.float32(1.0 / math.sqrt(length))
    cosine = np.cos(angle) * factor
    sine = np.sin(angle) * factor
    weight = np.where(modes == 0, 1.0, 2.0).astype(np.float32)[:, None]
    forward = np.stack([cosine, -sine])
    inverse = forward * weight
    group = np.arange(NB * half_z).reshape(NB, half_z)
    out = []
    for table, order in ((inverse, group), (forward, group.T)):
        m = SLOTS * order.reshape(1, -1, 1) + np.arange(SLOTS).reshape(-1, 1, 1)
        m = np.broadcast_to(m, (SLOTS, NB * half_z, 2)).reshape(-1)
        c = np.arange(m.size) % 2
        out.append((table[c, m].astype(ml_dtypes.bfloat16), m.astype(np.float32)))
    (inv, m_inv), (fwd, m_fwd) = out
    return inv, m_inv[:, None], np.ascontiguousarray(fwd.T), m_fwd[None, :]


def lat_consts(rows, n_z):
    freqs = np.arange(rows)
    phase = (freqs[:, None] * freqs[None, :]) % rows
    angle = phase.astype(np.float32) * np.float32(2.0 * math.pi / rows)
    factor = np.float32(1.0 / math.sqrt(rows))
    cosine = np.cos(angle) * factor
    sine = np.sin(angle) * factor
    top = np.stack([cosine, sine], axis=-1).reshape(rows, 2 * rows)
    low = np.stack([-sine, cosine], axis=-1).reshape(rows, 2 * rows)
    dft = np.concatenate([top, low], axis=0).astype(ml_dtypes.bfloat16)
    pick = np.zeros((n_z, NB, 2, 2, rows), np.float32)
    for x in range(NB):
        for core in range(2):
            for z in range(n_z):
                pick[z, x, core, :, (x * n_z + z) * 2 + core] = 2.0
    pick = pick.reshape(2 * rows, rows).astype(ml_dtypes.bfloat16)
    split = np.zeros((2, rows, rows, 2), np.float32)
    for part in range(2):
        split[part, np.arange(rows), np.arange(rows), part] = 1.0
    split = split.reshape(2 * rows, 2 * rows).astype(ml_dtypes.bfloat16)
    return dft, pick, split


def dot(a, b):
    return jnp.dot(a, b, preferred_element_type=F32)


def dot_nt(a, b):
    return lax.dot_general(a, b, (((1,), (1,)), ((), ())), preferred_element_type=F32)


def dot_tn(a, b):
    return lax.dot_general(a, b, (((0,), (0,)), ((), ())), preferred_element_type=F32)


def kernel(
    n_sec, n_z,
    go_h, inv_h, minv_h, assign_h, counts_h, sv_h, split_h, w1_h, b1_h, w2_h, pick_h, dft_h, fwd_h, mfwd_h,
    out_gi, out_w1, out_w2, out_b1,
    go, inv, minv, assign, counts, sv, split, w1, b1, w2, pick, dft, fwd, mfwd,
    send1, pencil, send2, band, gonext,
    quad1, quad2, vsend, vrecv, vcat, hid, slope, tab, tab2,
    wsend, wrecv,
    ld, s1, r1, sg, rg, s4, r4, sv_s, sv_r, sw, rw,
):
    rows = 8 * n_z
    half_z = n_z // 2
    jc = BS // (2 * n_z)
    sec = lax.axis_index("section")
    p = lax.axis_index("lat")
    x = p // (2 * n_z)
    z = lax.rem(p // 2, n_z)
    core = lax.rem(p, 2)
    odd = lax.rem(z, 2)
    block = 2 * odd + core
    line = 2 * x + core

    def at(xx, zz, cc):
        return xx * (2 * n_z) + zz * 2 + cc

    def signal(sem, section, device):
        pl.semaphore_signal(sem, inc=1, device_id=(section, device), device_id_type=MESH)

    def remote(src, dst, send, recv, section, device):
        return pltpu.make_async_remote_copy(
            src, dst, send, recv, device_id=(section, device), device_id_type=MESH
        )

    def wait_bytes(ref, sem):
        pltpu.make_async_copy(ref, ref, sem).wait()

    def far_first(i):
        half = (i + 1) // 2
        return lax.rem(z + n_z + half_z + jnp.where(lax.rem(i, 2) == 0, half, -half), n_z)

    line_up = [(2, 0), (2, 1), (1, 0), (1, 1), (3, 0), (3, 1), (0, 1), (0, 0)]
    plane = [(lax.rem(x + dx, NB), lax.rem(core + dc, 2)) for dx, dc in line_up]

    loads = [
        pltpu.make_async_copy(src, dst, ld.at[i])
        for i, (src, dst) in enumerate([
            (go_h, go), (inv_h, inv), (assign_h, assign), (counts_h, counts), (minv_h, minv), (sv_h, sv),
            (split_h, split), (w1_h, w1), (b1_h, b1), (w2_h, w2), (pick_h, pick), (dft_h, dft),
            (fwd_h, fwd), (mfwd_h, mfwd),
        ])
    ]
    for copy in loads[:5]:
        copy.start()

    barrier = pltpu.get_barrier_semaphore()

    def greet(i, carry):
        zz = far_first(i)
        for xx, cc in plane:
            signal(barrier, sec, at(xx, zz, cc))
        return carry

    lax.fori_loop(0, n_z - 1, greet, 0)
    for xx, cc in plane[:-1]:
        signal(barrier, sec, at(xx, z, cc))

    @pl.when(sec < n_sec - 1)
    def _():
        signal(barrier, sec + 1, p)

    for copy in loads[5:]:
        copy.start()

    for i in range(5):
        loads[i].wait()
    lane = lax.broadcasted_iota(jnp.int32, (1, rows), 1)
    own_band = jnp.sum(jnp.where(lane == p, assign[...], 0), axis=1, keepdims=True)
    count = jnp.sum(jnp.where(lane == own_band, counts[...], 0), axis=1, keepdims=True).astype(F32)
    modes = jnp.where(minv[...] < count, dot(inv[...], go[...]), 0.0)
    per_q = 8 * half_z
    lane_pad = jnp.zeros((per_q, LANES - BS), F32)
    for n in range(NB):
        for j in range(SLOTS):
            part = modes[j * per_q:(j + 1) * per_q, n * BS:(n + 1) * BS]
            part = jnp.concatenate([part, lane_pad], axis=1).astype(BF16)
            send1[:, n % 2, :, n // 2, j] = part.reshape(NB, half_z, 2, LANES)

    pl.semaphore_wait(barrier, rows - 1 + (sec > 0).astype(jnp.int32))

    def send_rows(zz, xx, cc):
        remote(
            send1.at[xx, cc, zz // 2, lax.rem(zz, 2)], pencil.at[8 * z + line], s1, r1, sec, at(xx, zz, cc)
        ).start()

    def spread(i, carry):
        for xx, cc in plane:
            send_rows(far_first(i), xx, cc)
        return carry

    lax.fori_loop(0, n_z - 1, spread, 0)
    for xx, cc in plane[:-1]:
        send_rows(z, xx, cc)
    pltpu.make_async_copy(send1.at[x, core, z // 2, odd], pencil.at[8 * z + line], r1).start()

    loads[5].wait()
    loads[6].wait()
    saved = dot(split[...], sv[...].reshape(2 * rows, SLOTS * BS))
    first = jnp.logical_and(
        lax.broadcasted_iota(jnp.int32, (2 * rows, LANES - BS), 1) == 0,
        lax.broadcasted_iota(jnp.int32, (2 * rows, LANES - BS), 0) < rows,
    )
    one = jnp.where(first, 1.0, 0.0).astype(F32)
    for j in range(SLOTS):
        vsend[j] = jnp.concatenate([saved[:, j * BS:(j + 1) * BS], one], axis=1).astype(BF16)
    for j in range(SLOTS):
        q, n = (SLOTS * block + j) // NB, lax.rem(SLOTS * block + j, NB)

        @pl.when(n == block)
        def _():
            pltpu.make_async_copy(vsend.at[j], vrecv.at[q], sv_r.at[q]).start()

        @pl.when(n != block)
        def _():
            remote(
                vsend.at[j], vrecv.at[q], sv_s.at[j], sv_r.at[q], sec, at(x, z - odd + n // 2, lax.rem(n, 2))
            ).start()

    @pl.when(sec > 0)
    def _():
        remote(go, gonext, sg, rg, sec - 1, p).start()

    for i in range(7, 14):
        loads[i].wait()
    row_id = lax.broadcasted_iota(jnp.int32, (LANES, LANES), 0)

    def padded(mat):
        mat = jnp.concatenate([mat.astype(F32), jnp.zeros((mat.shape[0], LANES - BS), F32)], axis=1)
        if mat.shape[0] == BS:
            mat = jnp.concatenate([mat, jnp.zeros((LANES - BS, LANES), F32)], axis=0)
        return mat

    for n in range(NB):
        lanes = slice(n * BS, (n + 1) * BS)

        @pl.when(block == n)
        def _():
            for src, dst in ((w1, quad1), (w2, quad2)):
                real, imag = padded(src[0, :, lanes]), padded(src[1, :, lanes])
                top_r, top_i = real, imag
                if src is w1:
                    bias = b1[...].astype(F32)
                    top_r = jnp.where(row_id == BS, padded(bias[0:1, lanes]), real)
                    top_i = jnp.where(row_id == BS, padded(bias[1:2, lanes]), imag)
                dst[0:LANES, 0:LANES] = top_r.astype(BF16)
                dst[0:LANES, LANES:] = top_i.astype(BF16)
                dst[LANES:, 0:LANES] = (-imag).astype(BF16)
                dst[LANES:, LANES:] = real.astype(BF16)

    bands = jnp.broadcast_to(assign[...].astype(F32), (8, rows)).astype(BF16)
    target = dot_nt(pick[...], bands)[:, 0:1]
    row_part = lax.rem(lax.broadcasted_iota(jnp.int32, (2 * rows, 1), 0), 2).astype(F32)
    column = lax.broadcasted_iota(jnp.int32, (2 * rows, 2 * rows), 1).astype(F32)
    chosen = jnp.where(column == target + row_part, 1.0, 0.0).astype(BF16)
    tab[...] = dot_nt(dft[...], chosen).astype(BF16)
    tab2[...] = dot_nt(chosen, dft[...]).astype(BF16)

    for q in range(SLOTS):
        wait_bytes(vrecv.at[q], sv_r.at[q])
        vcat[q * rows:(q + 1) * rows, 0:LANES] = vrecv[q, 0:rows]
        vcat[q * rows:(q + 1) * rows, LANES:] = vrecv[q, rows:]
    pre = dot(vcat[...], quad1[...])
    sig = jax.nn.sigmoid(pre)
    hid[...] = (pre * sig).astype(BF16)
    slope[...] = sig * (1.0 + pre * (1.0 - sig))

    wait_bytes(pencil, r1)

    spec = jnp.concatenate([pencil[:, j].reshape(2 * rows, LANES) for j in range(SLOTS)], axis=1)
    grad_y = dot(tab[...], spec).astype(BF16)
    dy = jnp.concatenate(
        [
            jnp.concatenate([grad_y[c * rows:(c + 1) * rows, j * LANES:(j + 1) * LANES] for c in range(2)], axis=1)
            for j in range(SLOTS)
        ],
        axis=0,
    )
    dp = (dot_nt(dy, quad2[...]) * slope[...]).astype(BF16)
    dv = dot_nt(dp, quad1[...]).astype(BF16)
    inner = jnp.concatenate(
        [
            jnp.concatenate([dv[j * rows:(j + 1) * rows, c * LANES:(c + 1) * LANES] for c in range(2)], axis=0)
            for j in range(SLOTS)
        ],
        axis=1,
    )
    grad_u = dot(tab2[...], inner).astype(BF16)
    for j in range(SLOTS):
        send2[:, j] = grad_u[:, j * LANES:(j + 1) * LANES].reshape(rows, 2, LANES)

    for w, (lhs, rhs) in enumerate(((dp, vcat), (dy, hid))):
        prod = dot_tn(lhs, rhs[...])
        real = prod[0:BS, 0:LANES] + prod[LANES:LANES + BS, LANES:]
        imag = prod[LANES:LANES + BS, 0:LANES] - prod[0:BS, LANES:]
        for c, val in enumerate((real, imag)):
            wsend[:, 2 * w + c] = val.astype(BF16).reshape(2 * n_z, jc, LANES)
    home = at(block, 0, 0)
    share = x * half_z + z // 2

    def back(zz, carry):
        for xx, cc in plane:
            remote(
                send2.at[8 * zz + 2 * xx + cc], band.at[z // 2, odd, x, core], s4, r4, sec - 1, at(xx, zz, cc)
            ).start()
        return carry

    def columns(to, carry):
        @pl.when(home + to != p)
        def _():
            remote(wsend.at[to], wrecv.at[share], sw, rw, sec, home + to).start()

        return carry

    def both(zz, carry):
        @pl.when(sec > 0)
        def _():
            back(zz, 0)

        columns(2 * zz, 0)
        columns(2 * zz + 1, 0)
        return carry

    lax.fori_loop(0, n_z, both, 0)

    @pl.when(x == block)
    def _():
        pltpu.make_async_copy(wsend.at[2 * z + core], wrecv.at[share], rw).start()

    @pl.when(sec < n_sec - 1)
    def _():
        wait_bytes(band, r4)
        wait_bytes(gonext, rg)
        blocks = []
        for n in range(NB):
            pieces = [band[:, n // 2, :, n % 2, j].reshape(per_q, LANES) for j in range(SLOTS)]
            blocks.append(jnp.concatenate(pieces, axis=0))
        table = jnp.where(mfwd[...] < count, fwd[...].astype(F32), 0.0).astype(BF16)
        mixed = dot(table, jnp.concatenate(blocks, axis=1))
        mixed = jnp.concatenate([mixed[:, n * LANES:n * LANES + BS] for n in range(NB)], axis=1)
        mixed = mixed.astype(BF16).astype(F32)
        out_gi[...] = (gonext[...].astype(F32) + mixed).astype(BF16)

    @pl.when(sec == n_sec - 1)
    def _():
        out_gi[...] = jnp.zeros_like(out_gi)

    wait_bytes(wrecv, rw)
    total = jnp.sum(wrecv[...].astype(F32), axis=0)
    out_w1[...] = total[0:2, :, 0:BS]
    out_w2[...] = total[2:4, :, 0:BS]
    flat = jnp.concatenate([total.reshape(4 * jc, LANES), jnp.zeros((LANES - 4 * jc, LANES), F32)], axis=0)
    flat = jnp.transpose(flat)
    for c in range(2):
        out_b1[c:c + 1, :] = flat[BS:BS + 1, c * jc:(c + 1) * jc]

    wait_bytes(pencil.at[pl.ds(0, rows - 1)], s1)

    @pl.when(sec > 0)
    def _():
        wait_bytes(band, s4)
        wait_bytes(gonext, sg)

    @pl.when(x == block)
    def _():
        wait_bytes(wsend.at[pl.ds(0, 2 * n_z - 1)], sw)

    @pl.when(x != block)
    def _():
        wait_bytes(wsend, sw)

    for j in range(SLOTS):
        @pl.when(lax.rem(SLOTS * block + j, NB) != block)
        def _():
            wait_bytes(vsend.at[j], sv_s.at[j])


def store(*refs):
    held, out, sems = refs[:4], refs[4:8], refs[8]
    copies = [pltpu.make_async_copy(held[i], out[i], sems.at[i]) for i in range(4)]
    for copy in copies:
        copy.start()
    for copy in copies:
        copy.wait()


def per_device(n_sec, n_lat, grad_out, spec_saved, w1, w2, b1, mode_counts, assignment):
    n_z = n_lat // 8
    half_z = n_z // 2
    rows = n_lat
    jc = BS // (2 * n_z)
    length, width = grad_out.shape[2:]
    n_modes = SLOTS * n_lat // NB
    inv, m_inv, fwd, m_fwd = lon_consts(n_modes, length, half_z)
    dft, pick, split = lat_consts(rows, n_z)
    operands = [
        grad_out.reshape(length, width), jnp.asarray(inv), jnp.asarray(m_inv), assignment.reshape(1, rows),
        mode_counts.reshape(1, rows), spec_saved.reshape(rows, 2, SLOTS * BS), jnp.asarray(split),
        w1.reshape(2, BS, width), b1.reshape(2, width), w2.reshape(2, BS, width), jnp.asarray(pick),
        jnp.asarray(dft), jnp.asarray(fwd), jnp.asarray(m_fwd),
    ]
    vmem = pltpu.VMEM
    tile = (SLOTS, 2, LANES)
    big = 2 * LANES
    scratch = [vmem(v.shape, v.dtype) for v in operands] + [
        vmem((NB, 2, half_z, 2) + tile, BF16),
        vmem((rows,) + tile, BF16),
        vmem((rows,) + tile, BF16),
        vmem((half_z, 2, NB, 2) + tile, BF16),
        vmem((length, width), BF16),
        vmem((big, big), BF16),
        vmem((big, big), BF16),
        vmem((SLOTS, 2 * rows, LANES), BF16),
        vmem((SLOTS, 2 * rows, LANES), BF16),
        vmem((SLOTS * rows, big), BF16),
        vmem((SLOTS * rows, big), BF16),
        vmem((SLOTS * rows, big), F32),
        vmem((2 * rows, 2 * rows), BF16),
        vmem((2 * rows, 2 * rows), BF16),
        vmem((2 * n_z, 4, jc, LANES), BF16),
        vmem((NB * half_z, 4, jc, LANES), BF16),
    ]
    dma = pltpu.SemaphoreType.DMA
    sems = [
        dma((14,)), dma(()), dma(()), dma(()), dma(()), dma(()), dma(()), dma((SLOTS,)), dma((SLOTS,)),
        dma(()), dma(()),
    ]
    hbm = pl.BlockSpec(memory_space=pl.ANY)
    whole = pl.BlockSpec(memory_space=pltpu.VMEM)
    held = pl.pallas_call(
        functools.partial(kernel, n_sec, n_z),
        out_shape=(
            vmem((length, width), BF16),
            vmem((2, jc, BS), F32),
            vmem((2, jc, BS), F32),
            vmem((2, jc), F32),
        ),
        in_specs=[hbm] * 14,
        out_specs=(whole,) * 4,
        scratch_shapes=scratch + sems,
        compiler_params=pltpu.CompilerParams(collective_id=0, has_side_effects=True),
        name="filter_backward",
    )(*operands)
    gi, gw1, gw2, gb1 = pl.pallas_call(
        store,
        out_shape=tuple(jax.ShapeDtypeStruct(v.shape, v.dtype) for v in held),
        in_specs=[hbm] * 4,
        out_specs=(hbm,) * 4,
        scratch_shapes=[dma((4,))],
        name="store",
    )(*[pltpu.with_memory_space_constraint(v, pltpu.VMEM) for v in held])
    return gi[None, None], jnp.swapaxes(gw1, 1, 2)[None], jnp.swapaxes(gw2, 1, 2)[None], gb1[None]


def solution(mesh):
    return jax.shard_map(
        functools.partial(per_device, mesh.shape["section"], mesh.shape["lat"]),
        mesh=mesh,
        in_specs=(
            P("section", "lat", None, None),
            P("section", None, None, "lat"),
            P("section", None, None, None),
            P("section", None, None, None),
            P("section", None, None),
            P(),
            P(),
        ),
        out_specs=(
            P("section", "lat", None, None),
            P("section", None, None, "lat"),
            P("section", None, None, "lat"),
            P("section", None, "lat"),
        ),
        check_vma=False,
    )
```

```python
import functools
import math

import jax
import jax.numpy as jnp
import ml_dtypes
import numpy as np
from jax import lax
from jax.experimental import pallas as pl
from jax.experimental.pallas import tpu as pltpu
from jax.sharding import PartitionSpec as P

NB = 4
BS = 96
LANES = 128
SLOTS = 3
F32 = jnp.float32
BF16 = jnp.bfloat16
MESH = pl.DeviceIdType.MESH


def lon_consts(n_modes, length, half_z):
    modes = np.arange(n_modes)
    phase = (modes[:, None] * np.arange(length)[None, :]) % length
    angle = phase.astype(np.float32) * np.float32(2.0 * math.pi / length)
    factor = np.float32(1.0 / math.sqrt(length))
    cosine = np.cos(angle) * factor
    sine = np.sin(angle) * factor
    weight = np.where(modes == 0, 1.0, 2.0).astype(np.float32)[:, None]
    forward = np.stack([cosine, -sine])
    inverse = forward * weight
    group = np.arange(NB * half_z).reshape(NB, half_z)
    out = []
    for table, order in ((inverse, group), (forward, group.T)):
        m = SLOTS * order.reshape(1, -1, 1) + np.arange(SLOTS).reshape(-1, 1, 1)
        m = np.broadcast_to(m, (SLOTS, NB * half_z, 2)).reshape(-1)
        c = np.arange(m.size) % 2
        out.append((table[c, m].astype(ml_dtypes.bfloat16), m.astype(np.float32)))
    (inv, m_inv), (fwd, m_fwd) = out
    return inv, m_inv[:, None], np.ascontiguousarray(fwd.T), m_fwd[None, :]


def lat_consts(rows, n_z):
    freqs = np.arange(rows)
    phase = (freqs[:, None] * freqs[None, :]) % rows
    angle = phase.astype(np.float32) * np.float32(2.0 * math.pi / rows)
    factor = np.float32(1.0 / math.sqrt(rows))
    cosine = np.cos(angle) * factor
    sine = np.sin(angle) * factor
    top = np.stack([cosine, sine], axis=-1).reshape(rows, 2 * rows)
    low = np.stack([-sine, cosine], axis=-1).reshape(rows, 2 * rows)
    dft = np.concatenate([top, low], axis=0).astype(ml_dtypes.bfloat16)
    pick = np.zeros((n_z, NB, 2, 2, rows), np.float32)
    for x in range(NB):
        for core in range(2):
            for z in range(n_z):
                pick[z, x, core, :, (x * n_z + z) * 2 + core] = 2.0
    pick = pick.reshape(2 * rows, rows).astype(ml_dtypes.bfloat16)
    split = np.zeros((2, rows, rows, 2), np.float32)
    for part in range(2):
        split[part, np.arange(rows), np.arange(rows), part] = 1.0
    split = split.reshape(2 * rows, 2 * rows).astype(ml_dtypes.bfloat16)
    return dft, pick, split


def dot(a, b):
    return jnp.dot(a, b, preferred_element_type=F32)


def dot_nt(a, b):
    return lax.dot_general(a, b, (((1,), (1,)), ((), ())), preferred_element_type=F32)


def dot_tn(a, b):
    return lax.dot_general(a, b, (((0,), (0,)), ((), ())), preferred_element_type=F32)


def kernel(
    n_sec, n_z,
    go_h, inv_h, minv_h, assign_h, counts_h, sv_h, split_h, w1_h, b1_h, w2_h, pick_h, dft_h, fwd_h, mfwd_h,
    out_gi, out_w1, out_w2, out_b1,
    go, inv, minv, assign, counts, sv, split, w1, b1, w2, pick, dft, fwd, mfwd,
    send1, pencil, send2, band, gonext,
    quad1, quad2, vsend, vrecv, vcat, hid, slope, tab, tab2,
    wsend, wrecv,
    ld, s1, r1, sg, rg, s4, r4, sv_s, sv_r, sw, rw, late_sem, all_sem,
):
    rows = 8 * n_z
    half_z = n_z // 2
    jc = BS // (2 * n_z)
    first_late = n_z - 2
    sec = lax.axis_index("section")
    p = lax.axis_index("lat")
    x = p // (2 * n_z)
    z = lax.rem(p // 2, n_z)
    core = lax.rem(p, 2)
    odd = lax.rem(z, 2)
    block = 2 * odd + core
    line = 2 * x + core

    def at(xx, zz, cc):
        return xx * (2 * n_z) + zz * 2 + cc

    def signal(sem, section, device):
        pl.semaphore_signal(sem, inc=1, device_id=(section, device), device_id_type=MESH)

    def remote(src, dst, send, recv, section, device):
        return pltpu.make_async_remote_copy(
            src, dst, send, recv, device_id=(section, device), device_id_type=MESH
        )

    def wait_bytes(ref, sem):
        pltpu.make_async_copy(ref, ref, sem).wait()

    def far_first(i):
        half = (i + 1) // 2
        return lax.rem(z + n_z + half_z + jnp.where(lax.rem(i, 2) == 0, half, -half), n_z)

    line_up = [(2, 0), (2, 1), (1, 0), (1, 1), (3, 0), (3, 1), (0, 1), (0, 0)]
    plane = [(lax.rem(x + dx, NB), lax.rem(core + dc, 2)) for dx, dc in line_up]

    loads = [
        pltpu.make_async_copy(src, dst, ld.at[i])
        for i, (src, dst) in enumerate([
            (go_h, go), (inv_h, inv), (assign_h, assign), (counts_h, counts), (minv_h, minv), (sv_h, sv),
            (split_h, split), (w1_h, w1), (b1_h, b1), (w2_h, w2), (pick_h, pick), (dft_h, dft),
            (fwd_h, fwd), (mfwd_h, mfwd),
        ])
    ]
    for copy in loads[:5]:
        copy.start()

    barrier = pltpu.get_barrier_semaphore()
    late = z >= first_late
    n_early = 8 * first_late
    n_late = rows - n_early
    from_y = (sec > 0).astype(jnp.int32)

    @pl.when(sec < n_sec - 1)
    def _():
        signal(barrier, sec + 1, p)

    def greet(sem, zz):
        for xx, cc in plane:
            signal(sem, sec, at(xx, zz, cc))

    @pl.when(jnp.logical_not(late))
    def _():
        def greet_all(i, carry):
            greet(barrier, far_first(i))
            return carry

        lax.fori_loop(0, n_z - 1, greet_all, 0)
        for xx, cc in plane[:-1]:
            signal(barrier, sec, at(xx, z, cc))

    for copy in loads[5:]:
        copy.start()

    @pl.when(late)
    def _():
        pl.semaphore_wait(barrier, n_early + from_y)

        def here(i, carry):
            zz = far_first(i)

            @pl.when(zz < first_late)
            def _():
                greet(late_sem, zz)

            return carry

        lax.fori_loop(0, n_z, here, 0)

    for i in range(5):
        loads[i].wait()
    lane = lax.broadcasted_iota(jnp.int32, (1, rows), 1)
    own_band = jnp.sum(jnp.where(lane == p, assign[...], 0), axis=1, keepdims=True)
    count = jnp.sum(jnp.where(lane == own_band, counts[...], 0), axis=1, keepdims=True).astype(F32)
    modes = jnp.where(minv[...] < count, dot(inv[...], go[...]), 0.0)
    per_q = 8 * half_z
    lane_pad = jnp.zeros((per_q, LANES - BS), F32)
    for n in range(NB):
        for j in range(SLOTS):
            part = modes[j * per_q:(j + 1) * per_q, n * BS:(n + 1) * BS]
            part = jnp.concatenate([part, lane_pad], axis=1).astype(BF16)
            send1[:, n % 2, :, n // 2, j] = part.reshape(NB, half_z, 2, LANES)

    @pl.when(jnp.logical_not(late))
    def _():
        pl.semaphore_wait(barrier, n_early - 1 + from_y)

    def send_rows(zz, xx, cc):
        remote(
            send1.at[xx, cc, zz // 2, lax.rem(zz, 2)], pencil.at[8 * z + line], s1, r1, sec, at(xx, zz, cc)
        ).start()

    def spread(to_late):
        def step(i, carry):
            zz = far_first(i)

            @pl.when(zz >= first_late if to_late else zz < first_late)
            def _():
                for xx, cc in plane:
                    send_rows(zz, xx, cc)

            return carry

        lax.fori_loop(0, n_z - 1, step, 0)

    spread(False)

    @pl.when(late)
    def _():
        pl.semaphore_wait(all_sem, 1)
        spread(True)

    for xx, cc in plane[:-1]:
        send_rows(z, xx, cc)
    pltpu.make_async_copy(send1.at[x, core, z // 2, odd], pencil.at[8 * z + line], r1).start()

    loads[5].wait()
    loads[6].wait()
    saved = dot(split[...], sv[...].reshape(2 * rows, SLOTS * BS))
    first = jnp.logical_and(
        lax.broadcasted_iota(jnp.int32, (2 * rows, LANES - BS), 1) == 0,
        lax.broadcasted_iota(jnp.int32, (2 * rows, LANES - BS), 0) < rows,
    )
    one = jnp.where(first, 1.0, 0.0).astype(F32)
    for j in range(SLOTS):
        vsend[j] = jnp.concatenate([saved[:, j * BS:(j + 1) * BS], one], axis=1).astype(BF16)
    for j in range(SLOTS):
        q, n = (SLOTS * block + j) // NB, lax.rem(SLOTS * block + j, NB)

        @pl.when(n == block)
        def _():
            pltpu.make_async_copy(vsend.at[j], vrecv.at[q], sv_r.at[q]).start()

        @pl.when(n != block)
        def _():
            remote(
                vsend.at[j], vrecv.at[q], sv_s.at[j], sv_r.at[q], sec, at(x, z - odd + n // 2, lax.rem(n, 2))
            ).start()

    @pl.when(sec > 0)
    def _():
        remote(go, gonext, sg, rg, sec - 1, p).start()

    @pl.when(jnp.logical_not(late))
    def _():
        pl.semaphore_wait(late_sem, n_late)

        @pl.when(z == first_late - 1)
        def _():
            for zz in range(first_late, n_z):
                signal(all_sem, sec, at(x, zz, core))

        spread(True)

    for i in range(7, 14):
        loads[i].wait()
    row_id = lax.broadcasted_iota(jnp.int32, (LANES, LANES), 0)

    def padded(mat):
        mat = jnp.concatenate([mat.astype(F32), jnp.zeros((mat.shape[0], LANES - BS), F32)], axis=1)
        if mat.shape[0] == BS:
            mat = jnp.concatenate([mat, jnp.zeros((LANES - BS, LANES), F32)], axis=0)
        return mat

    for n in range(NB):
        lanes = slice(n * BS, (n + 1) * BS)

        @pl.when(block == n)
        def _():
            for src, dst in ((w1, quad1), (w2, quad2)):
                real, imag = padded(src[0, :, lanes]), padded(src[1, :, lanes])
                top_r, top_i = real, imag
                if src is w1:
                    bias = b1[...].astype(F32)
                    top_r = jnp.where(row_id == BS, padded(bias[0:1, lanes]), real)
                    top_i = jnp.where(row_id == BS, padded(bias[1:2, lanes]), imag)
                dst[0:LANES, 0:LANES] = top_r.astype(BF16)
                dst[0:LANES, LANES:] = top_i.astype(BF16)
                dst[LANES:, 0:LANES] = (-imag).astype(BF16)
                dst[LANES:, LANES:] = real.astype(BF16)

    bands = jnp.broadcast_to(assign[...].astype(F32), (8, rows)).astype(BF16)
    target = dot_nt(pick[...], bands)[:, 0:1]
    row_part = lax.rem(lax.broadcasted_iota(jnp.int32, (2 * rows, 1), 0), 2).astype(F32)
    column = lax.broadcasted_iota(jnp.int32, (2 * rows, 2 * rows), 1).astype(F32)
    chosen = jnp.where(column == target + row_part, 1.0, 0.0).astype(BF16)
    tab[...] = dot_nt(dft[...], chosen).astype(BF16)
    tab2[...] = dot_nt(chosen, dft[...]).astype(BF16)

    for q in range(SLOTS):
        wait_bytes(vrecv.at[q], sv_r.at[q])
        vcat[q * rows:(q + 1) * rows, 0:LANES] = vrecv[q, 0:rows]
        vcat[q * rows:(q + 1) * rows, LANES:] = vrecv[q, rows:]
    pre = dot(vcat[...], quad1[...])
    sig = jax.nn.sigmoid(pre)
    hid[...] = (pre * sig).astype(BF16)
    slope[...] = sig * (1.0 + pre * (1.0 - sig))

    wait_bytes(pencil, r1)

    spec = jnp.concatenate([pencil[:, j].reshape(2 * rows, LANES) for j in range(SLOTS)], axis=1)
    grad_y = dot(tab[...], spec).astype(BF16)
    dy = jnp.concatenate(
        [
            jnp.concatenate([grad_y[c * rows:(c + 1) * rows, j * LANES:(j + 1) * LANES] for c in range(2)], axis=1)
            for j in range(SLOTS)
        ],
        axis=0,
    )
    dp = (dot_nt(dy, quad2[...]) * slope[...]).astype(BF16)
    dv = dot_nt(dp, quad1[...]).astype(BF16)
    inner = jnp.concatenate(
        [
            jnp.concatenate([dv[j * rows:(j + 1) * rows, c * LANES:(c + 1) * LANES] for c in range(2)], axis=0)
            for j in range(SLOTS)
        ],
        axis=1,
    )
    grad_u = dot(tab2[...], inner).astype(BF16)
    for j in range(SLOTS):
        send2[:, j] = grad_u[:, j * LANES:(j + 1) * LANES].reshape(rows, 2, LANES)

    for w, (lhs, rhs) in enumerate(((dp, vcat), (dy, hid))):
        prod = dot_tn(lhs, rhs[...])
        real = prod[0:BS, 0:LANES] + prod[LANES:LANES + BS, LANES:]
        imag = prod[LANES:LANES + BS, 0:LANES] - prod[0:BS, LANES:]
        for c, val in enumerate((real, imag)):
            wsend[:, 2 * w + c] = val.astype(BF16).reshape(2 * n_z, jc, LANES)
    home = at(block, 0, 0)
    share = x * half_z + z // 2

    def back(zz, carry):
        for xx, cc in plane:
            remote(
                send2.at[8 * zz + 2 * xx + cc], band.at[z // 2, odd, x, core], s4, r4, sec - 1, at(xx, zz, cc)
            ).start()
        return carry

    def columns(to, carry):
        @pl.when(home + to != p)
        def _():
            remote(wsend.at[to], wrecv.at[share], sw, rw, sec, home + to).start()

        return carry

    def both(zz, carry):
        @pl.when(sec > 0)
        def _():
            back(zz, 0)

        columns(2 * zz, 0)
        columns(2 * zz + 1, 0)
        return carry

    lax.fori_loop(0, n_z, both, 0)

    @pl.when(x == block)
    def _():
        pltpu.make_async_copy(wsend.at[2 * z + core], wrecv.at[share], rw).start()

    @pl.when(sec < n_sec - 1)
    def _():
        wait_bytes(band, r4)
        wait_bytes(gonext, rg)
        blocks = []
        for n in range(NB):
            pieces = [band[:, n // 2, :, n % 2, j].reshape(per_q, LANES) for j in range(SLOTS)]
            blocks.append(jnp.concatenate(pieces, axis=0))
        table = jnp.where(mfwd[...] < count, fwd[...].astype(F32), 0.0).astype(BF16)
        mixed = dot(table, jnp.concatenate(blocks, axis=1))
        mixed = jnp.concatenate([mixed[:, n * LANES:n * LANES + BS] for n in range(NB)], axis=1)
        mixed = mixed.astype(BF16).astype(F32)
        out_gi[...] = (gonext[...].astype(F32) + mixed).astype(BF16)

    @pl.when(sec == n_sec - 1)
    def _():
        out_gi[...] = jnp.zeros_like(out_gi)

    wait_bytes(wrecv, rw)
    total = jnp.sum(wrecv[...].astype(F32), axis=0)
    out_w1[...] = total[0:2, :, 0:BS]
    out_w2[...] = total[2:4, :, 0:BS]
    bias_lane = lax.broadcasted_iota(jnp.int32, (2, jc, LANES), 2) == BS
    out_b1[...] = jnp.sum(jnp.where(bias_lane, total[0:2], 0.0), axis=2)

    wait_bytes(pencil.at[pl.ds(0, rows - 1)], s1)

    @pl.when(sec > 0)
    def _():
        wait_bytes(band, s4)
        wait_bytes(gonext, sg)

    @pl.when(x == block)
    def _():
        wait_bytes(wsend.at[pl.ds(0, 2 * n_z - 1)], sw)

    @pl.when(x != block)
    def _():
        wait_bytes(wsend, sw)

    for j in range(SLOTS):
        @pl.when(lax.rem(SLOTS * block + j, NB) != block)
        def _():
            wait_bytes(vsend.at[j], sv_s.at[j])


def store(*refs):
    held, out, sems = refs[:4], refs[4:8], refs[8]
    copies = [pltpu.make_async_copy(held[i], out[i], sems.at[i]) for i in range(4)]
    for copy in copies:
        copy.start()
    for copy in copies:
        copy.wait()


def per_device(n_sec, n_lat, grad_out, spec_saved, w1, w2, b1, mode_counts, assignment):
    n_z = n_lat // 8
    half_z = n_z // 2
    rows = n_lat
    jc = BS // (2 * n_z)
    length, width = grad_out.shape[2:]
    n_modes = SLOTS * n_lat // NB
    inv, m_inv, fwd, m_fwd = lon_consts(n_modes, length, half_z)
    dft, pick, split = lat_consts(rows, n_z)
    operands = [
        grad_out.reshape(length, width), jnp.asarray(inv), jnp.asarray(m_inv), assignment.reshape(1, rows),
        mode_counts.reshape(1, rows), spec_saved.reshape(rows, 2, SLOTS * BS), jnp.asarray(split),
        w1.reshape(2, BS, width), b1.reshape(2, width), w2.reshape(2, BS, width), jnp.asarray(pick),
        jnp.asarray(dft), jnp.asarray(fwd), jnp.asarray(m_fwd),
    ]
    vmem = pltpu.VMEM
    tile = (SLOTS, 2, LANES)
    big = 2 * LANES
    scratch = [vmem(v.shape, v.dtype) for v in operands] + [
        vmem((NB, 2, half_z, 2) + tile, BF16),
        vmem((rows,) + tile, BF16),
        vmem((rows,) + tile, BF16),
        vmem((half_z, 2, NB, 2) + tile, BF16),
        vmem((length, width), BF16),
        vmem((big, big), BF16),
        vmem((big, big), BF16),
        vmem((SLOTS, 2 * rows, LANES), BF16),
        vmem((SLOTS, 2 * rows, LANES), BF16),
        vmem((SLOTS * rows, big), BF16),
        vmem((SLOTS * rows, big), BF16),
        vmem((SLOTS * rows, big), F32),
        vmem((2 * rows, 2 * rows), BF16),
        vmem((2 * rows, 2 * rows), BF16),
        vmem((2 * n_z, 4, jc, LANES), BF16),
        vmem((NB * half_z, 4, jc, LANES), BF16),
    ]
    dma = pltpu.SemaphoreType.DMA
    sems = [
        dma((14,)), dma(()), dma(()), dma(()), dma(()), dma(()), dma(()), dma((SLOTS,)), dma((SLOTS,)),
        dma(()), dma(()), pltpu.SemaphoreType.REGULAR, pltpu.SemaphoreType.REGULAR,
    ]
    hbm = pl.BlockSpec(memory_space=pl.ANY)
    whole = pl.BlockSpec(memory_space=pltpu.VMEM)
    held = pl.pallas_call(
        functools.partial(kernel, n_sec, n_z),
        out_shape=(
            vmem((length, width), BF16),
            vmem((2, jc, BS), F32),
            vmem((2, jc, BS), F32),
            vmem((2, jc), F32),
        ),
        in_specs=[hbm] * 14,
        out_specs=(whole,) * 4,
        scratch_shapes=scratch + sems,
        compiler_params=pltpu.CompilerParams(collective_id=0, has_side_effects=True),
        name="filter_backward",
    )(*operands)
    gi, gw1, gw2, gb1 = pl.pallas_call(
        store,
        out_shape=tuple(jax.ShapeDtypeStruct(v.shape, v.dtype) for v in held),
        in_specs=[hbm] * 4,
        out_specs=(hbm,) * 4,
        scratch_shapes=[dma((4,))],
        name="store",
    )(*[pltpu.with_memory_space_constraint(v, pltpu.VMEM) for v in held])
    return gi[None, None], jnp.swapaxes(gw1, 1, 2)[None], jnp.swapaxes(gw2, 1, 2)[None], gb1[None]


def solution(mesh):
    return jax.shard_map(
        functools.partial(per_device, mesh.shape["section"], mesh.shape["lat"]),
        mesh=mesh,
        in_specs=(
            P("section", "lat", None, None),
            P("section", None, None, "lat"),
            P("section", None, None, None),
            P("section", None, None, None),
            P("section", None, None),
            P(),
            P(),
        ),
        out_specs=(
            P("section", "lat", None, None),
            P("section", None, None, "lat"),
            P("section", None, None, "lat"),
            P("section", None, "lat"),
        ),
        check_vma=False,
    )
```

```python
import functools
import math

import jax
import jax.numpy as jnp
import ml_dtypes
import numpy as np
from jax import lax
from jax.experimental import pallas as pl
from jax.experimental.pallas import tpu as pltpu
from jax.sharding import PartitionSpec as P

NB = 4
BS = 96
LANES = 128
SLOTS = 3
F32 = jnp.float32
BF16 = jnp.bfloat16
MESH = pl.DeviceIdType.MESH


def lon_consts(n_modes, length, half_z):
    modes = np.arange(n_modes)
    phase = (modes[:, None] * np.arange(length)[None, :]) % length
    angle = phase.astype(np.float32) * np.float32(2.0 * math.pi / length)
    factor = np.float32(1.0 / math.sqrt(length))
    cosine = np.cos(angle) * factor
    sine = np.sin(angle) * factor
    weight = np.where(modes == 0, 1.0, 2.0).astype(np.float32)[:, None]
    forward = np.stack([cosine, -sine])
    inverse = forward * weight
    group = np.arange(NB * half_z).reshape(NB, half_z)
    out = []
    for table, order in ((inverse, group), (forward, group.T)):
        m = SLOTS * order.reshape(1, -1, 1) + np.arange(SLOTS).reshape(-1, 1, 1)
        m = np.broadcast_to(m, (SLOTS, NB * half_z, 2)).reshape(-1)
        c = np.arange(m.size) % 2
        out.append((table[c, m].astype(ml_dtypes.bfloat16), m.astype(np.float32)))
    (inv, m_inv), (fwd, m_fwd) = out
    return inv, m_inv[:, None], np.ascontiguousarray(fwd.T), m_fwd[None, :]


def lat_consts(rows, n_z):
    freqs = np.arange(rows)
    phase = (freqs[:, None] * freqs[None, :]) % rows
    angle = phase.astype(np.float32) * np.float32(2.0 * math.pi / rows)
    factor = np.float32(1.0 / math.sqrt(rows))
    cosine = np.cos(angle) * factor
    sine = np.sin(angle) * factor
    top = np.stack([cosine, sine], axis=-1).reshape(rows, 2 * rows)
    low = np.stack([-sine, cosine], axis=-1).reshape(rows, 2 * rows)
    dft = np.concatenate([top, low], axis=0).astype(ml_dtypes.bfloat16)
    pick = np.zeros((n_z, NB, 2, 2, rows), np.float32)
    for x in range(NB):
        for core in range(2):
            for z in range(n_z):
                pick[z, x, core, :, (x * n_z + z) * 2 + core] = 2.0
    pick = pick.reshape(2 * rows, rows).astype(ml_dtypes.bfloat16)
    split = np.zeros((2, rows, rows, 2), np.float32)
    for part in range(2):
        split[part, np.arange(rows), np.arange(rows), part] = 1.0
    split = split.reshape(2 * rows, 2 * rows).astype(ml_dtypes.bfloat16)
    return dft, pick, split


def dot(a, b):
    return jnp.dot(a, b, preferred_element_type=F32)


def dot_nt(a, b):
    return lax.dot_general(a, b, (((1,), (1,)), ((), ())), preferred_element_type=F32)


def dot_tn(a, b):
    return lax.dot_general(a, b, (((0,), (0,)), ((), ())), preferred_element_type=F32)


def kernel(
    n_sec, n_z,
    go_h, inv_h, minv_h, assign_h, counts_h, sv_h, split_h, w1_h, b1_h, w2_h, pick_h, dft_h, fwd_h, mfwd_h,
    out_gi, out_w1, out_w2, out_b1,
    go, inv, minv, assign, counts, sv, split, w1, b1, w2, pick, dft, fwd, mfwd,
    send1, pencil, send2, band, gonext,
    quad1, quad2, vsend, vrecv, vcat, hid, slope, tab, tab2,
    wsend, wrecv,
    ld, s1, r1, sg, rg, s4, r4, sv_s, sv_r, sw, rw,
):
    rows = 8 * n_z
    half_z = n_z // 2
    jc = BS // (2 * n_z)
    sec = lax.axis_index("section")
    p = lax.axis_index("lat")
    x = p // (2 * n_z)
    z = lax.rem(p // 2, n_z)
    core = lax.rem(p, 2)
    odd = lax.rem(z, 2)
    block = 2 * odd + core
    line = 2 * x + core

    def at(xx, zz, cc):
        return xx * (2 * n_z) + zz * 2 + cc

    def signal(sem, section, device):
        pl.semaphore_signal(sem, inc=1, device_id=(section, device), device_id_type=MESH)

    def remote(src, dst, send, recv, section, device):
        return pltpu.make_async_remote_copy(
            src, dst, send, recv, device_id=(section, device), device_id_type=MESH
        )

    def wait_bytes(ref, sem):
        pltpu.make_async_copy(ref, ref, sem).wait()

    def far_first(i):
        half = (i + 1) // 2
        return lax.rem(z + n_z + half_z + jnp.where(lax.rem(i, 2) == 0, half, -half), n_z)

    line_up = [(2, 0), (2, 1), (1, 0), (1, 1), (3, 0), (3, 1), (0, 1), (0, 0)]
    plane = [(lax.rem(x + dx, NB), lax.rem(core + dc, 2)) for dx, dc in line_up]

    loads = [
        pltpu.make_async_copy(src, dst, ld.at[i])
        for i, (src, dst) in enumerate([
            (go_h, go), (inv_h, inv), (assign_h, assign), (counts_h, counts), (minv_h, minv), (sv_h, sv),
            (split_h, split), (w1_h, w1), (b1_h, b1), (w2_h, w2), (pick_h, pick), (dft_h, dft),
            (fwd_h, fwd), (mfwd_h, mfwd),
        ])
    ]
    barrier = pltpu.get_barrier_semaphore()

    def greet(i, carry):
        zz = far_first(i)
        for xx, cc in plane:
            signal(barrier, sec, at(xx, zz, cc))
        return carry

    lax.fori_loop(0, n_z - 1, greet, 0)
    for xx, cc in plane[:-1]:
        signal(barrier, sec, at(xx, z, cc))

    @pl.when(sec < n_sec - 1)
    def _():
        signal(barrier, sec + 1, p)

    for copy in loads:
        copy.start()

    for i in range(5):
        loads[i].wait()
    lane = lax.broadcasted_iota(jnp.int32, (1, rows), 1)
    own_band = jnp.sum(jnp.where(lane == p, assign[...], 0), axis=1, keepdims=True)
    count = jnp.sum(jnp.where(lane == own_band, counts[...], 0), axis=1, keepdims=True).astype(F32)
    modes = jnp.where(minv[...] < count, dot(inv[...], go[...]), 0.0)
    per_q = 8 * half_z
    lane_pad = jnp.zeros((per_q, LANES - BS), F32)
    for n in range(NB):
        for j in range(SLOTS):
            part = modes[j * per_q:(j + 1) * per_q, n * BS:(n + 1) * BS]
            part = jnp.concatenate([part, lane_pad], axis=1).astype(BF16)
            send1[:, n % 2, :, n // 2, j] = part.reshape(NB, half_z, 2, LANES)

    pl.semaphore_wait(barrier, rows - 1 + (sec > 0).astype(jnp.int32))

    def send_rows(zz, xx, cc):
        remote(
            send1.at[xx, cc, zz // 2, lax.rem(zz, 2)], pencil.at[8 * z + line], s1, r1, sec, at(xx, zz, cc)
        ).start()

    def spread(i, carry):
        for xx, cc in plane:
            send_rows(far_first(i), xx, cc)
        return carry

    lax.fori_loop(0, n_z - 1, spread, 0)
    for xx, cc in plane[:-1]:
        send_rows(z, xx, cc)
    pltpu.make_async_copy(send1.at[x, core, z // 2, odd], pencil.at[8 * z + line], r1).start()

    loads[5].wait()
    loads[6].wait()
    saved = dot(split[...], sv[...].reshape(2 * rows, SLOTS * BS))
    first = jnp.logical_and(
        lax.broadcasted_iota(jnp.int32, (2 * rows, LANES - BS), 1) == 0,
        lax.broadcasted_iota(jnp.int32, (2 * rows, LANES - BS), 0) < rows,
    )
    one = jnp.where(first, 1.0, 0.0).astype(F32)
    for j in range(SLOTS):
        vsend[j] = jnp.concatenate([saved[:, j * BS:(j + 1) * BS], one], axis=1).astype(BF16)
    for j in range(SLOTS):
        q, n = (SLOTS * block + j) // NB, lax.rem(SLOTS * block + j, NB)

        @pl.when(n == block)
        def _():
            pltpu.make_async_copy(vsend.at[j], vrecv.at[q], sv_r.at[q]).start()

        @pl.when(n != block)
        def _():
            remote(
                vsend.at[j], vrecv.at[q], sv_s.at[j], sv_r.at[q], sec, at(x, z - odd + n // 2, lax.rem(n, 2))
            ).start()

    @pl.when(sec > 0)
    def _():
        remote(go, gonext, sg, rg, sec - 1, p).start()

    for i in range(7, 14):
        loads[i].wait()
    row_id = lax.broadcasted_iota(jnp.int32, (LANES, LANES), 0)

    def padded(mat):
        mat = jnp.concatenate([mat.astype(F32), jnp.zeros((mat.shape[0], LANES - BS), F32)], axis=1)
        if mat.shape[0] == BS:
            mat = jnp.concatenate([mat, jnp.zeros((LANES - BS, LANES), F32)], axis=0)
        return mat

    for n in range(NB):
        lanes = slice(n * BS, (n + 1) * BS)

        @pl.when(block == n)
        def _():
            for src, dst in ((w1, quad1), (w2, quad2)):
                real, imag = padded(src[0, :, lanes]), padded(src[1, :, lanes])
                top_r, top_i = real, imag
                if src is w1:
                    bias = b1[...].astype(F32)
                    top_r = jnp.where(row_id == BS, padded(bias[0:1, lanes]), real)
                    top_i = jnp.where(row_id == BS, padded(bias[1:2, lanes]), imag)
                dst[0:LANES, 0:LANES] = top_r.astype(BF16)
                dst[0:LANES, LANES:] = top_i.astype(BF16)
                dst[LANES:, 0:LANES] = (-imag).astype(BF16)
                dst[LANES:, LANES:] = real.astype(BF16)

    bands = jnp.broadcast_to(assign[...].astype(F32), (8, rows)).astype(BF16)
    target = dot_nt(pick[...], bands)[:, 0:1]
    row_part = lax.rem(lax.broadcasted_iota(jnp.int32, (2 * rows, 1), 0), 2).astype(F32)
    column = lax.broadcasted_iota(jnp.int32, (2 * rows, 2 * rows), 1).astype(F32)
    chosen = jnp.where(column == target + row_part, 1.0, 0.0).astype(BF16)
    tab[...] = dot_nt(dft[...], chosen).astype(BF16)
    tab2[...] = dot_nt(chosen, dft[...]).astype(BF16)

    for q in range(SLOTS):
        wait_bytes(vrecv.at[q], sv_r.at[q])
        vcat[q * rows:(q + 1) * rows, 0:LANES] = vrecv[q, 0:rows]
        vcat[q * rows:(q + 1) * rows, LANES:] = vrecv[q, rows:]
    pre = dot(vcat[...], quad1[...])
    sig = jax.nn.sigmoid(pre)
    hid[...] = (pre * sig).astype(BF16)
    slope[...] = sig * (1.0 + pre * (1.0 - sig))

    wait_bytes(pencil, r1)

    spec = jnp.concatenate([pencil[:, j].reshape(2 * rows, LANES) for j in range(SLOTS)], axis=1)
    grad_y = dot(tab[...], spec).astype(BF16)
    dy = jnp.concatenate(
        [
            jnp.concatenate([grad_y[c * rows:(c + 1) * rows, j * LANES:(j + 1) * LANES] for c in range(2)], axis=1)
            for j in range(SLOTS)
        ],
        axis=0,
    )
    dp = (dot_nt(dy, quad2[...]) * slope[...]).astype(BF16)
    dv = dot_nt(dp, quad1[...]).astype(BF16)
    inner = jnp.concatenate(
        [
            jnp.concatenate([dv[j * rows:(j + 1) * rows, c * LANES:(c + 1) * LANES] for c in range(2)], axis=0)
            for j in range(SLOTS)
        ],
        axis=1,
    )
    grad_u = dot(tab2[...], inner).astype(BF16)
    for j in range(SLOTS):
        send2[:, j] = grad_u[:, j * LANES:(j + 1) * LANES].reshape(rows, 2, LANES)

    for w, (lhs, rhs) in enumerate(((dp, vcat), (dy, hid))):
        prod = dot_tn(lhs, rhs[...])
        real = prod[0:BS, 0:LANES] + prod[LANES:LANES + BS, LANES:]
        imag = prod[LANES:LANES + BS, 0:LANES] - prod[0:BS, LANES:]
        for c, val in enumerate((real, imag)):
            wsend[:, 2 * w + c] = val.astype(BF16).reshape(2 * n_z, jc, LANES)
    home = at(block, 0, 0)
    share = x * half_z + z // 2

    def back(zz, carry):
        for xx, cc in plane:
            remote(
                send2.at[8 * zz + 2 * xx + cc], band.at[z // 2, odd, x, core], s4, r4, sec - 1, at(xx, zz, cc)
            ).start()
        return carry

    def columns(to, carry):
        @pl.when(home + to != p)
        def _():
            remote(wsend.at[to], wrecv.at[share], sw, rw, sec, home + to).start()

        return carry

    def both(zz, carry):
        @pl.when(sec > 0)
        def _():
            back(zz, 0)

        columns(2 * zz, 0)
        columns(2 * zz + 1, 0)
        return carry

    lax.fori_loop(0, n_z, both, 0)

    @pl.when(x == block)
    def _():
        pltpu.make_async_copy(wsend.at[2 * z + core], wrecv.at[share], rw).start()

    @pl.when(sec < n_sec - 1)
    def _():
        wait_bytes(band, r4)
        wait_bytes(gonext, rg)
        blocks = []
        for n in range(NB):
            pieces = [band[:, n // 2, :, n % 2, j].reshape(per_q, LANES) for j in range(SLOTS)]
            blocks.append(jnp.concatenate(pieces, axis=0))
        table = jnp.where(mfwd[...] < count, fwd[...].astype(F32), 0.0).astype(BF16)
        mixed = dot(table, jnp.concatenate(blocks, axis=1))
        mixed = jnp.concatenate([mixed[:, n * LANES:n * LANES + BS] for n in range(NB)], axis=1)
        mixed = mixed.astype(BF16).astype(F32)
        out_gi[...] = (gonext[...].astype(F32) + mixed).astype(BF16)

    @pl.when(sec == n_sec - 1)
    def _():
        out_gi[...] = jnp.zeros_like(out_gi)

    wait_bytes(wrecv, rw)
    total = jnp.sum(wrecv[...].astype(F32), axis=0)
    out_w1[...] = total[0:2, :, 0:BS]
    out_w2[...] = total[2:4, :, 0:BS]
    bias_lane = lax.broadcasted_iota(jnp.int32, (2, jc, LANES), 2) == BS
    out_b1[...] = jnp.sum(jnp.where(bias_lane, total[0:2], 0.0), axis=2)

    wait_bytes(pencil.at[pl.ds(0, rows - 1)], s1)

    @pl.when(sec > 0)
    def _():
        wait_bytes(band, s4)
        wait_bytes(gonext, sg)

    @pl.when(x == block)
    def _():
        wait_bytes(wsend.at[pl.ds(0, 2 * n_z - 1)], sw)

    @pl.when(x != block)
    def _():
        wait_bytes(wsend, sw)

    for j in range(SLOTS):
        @pl.when(lax.rem(SLOTS * block + j, NB) != block)
        def _():
            wait_bytes(vsend.at[j], sv_s.at[j])


def store(*refs):
    held, out, sems = refs[:4], refs[4:8], refs[8]
    copies = [pltpu.make_async_copy(held[i], out[i], sems.at[i]) for i in range(4)]
    for copy in copies:
        copy.start()
    for copy in copies:
        copy.wait()


def per_device(n_sec, n_lat, grad_out, spec_saved, w1, w2, b1, mode_counts, assignment):
    n_z = n_lat // 8
    half_z = n_z // 2
    rows = n_lat
    jc = BS // (2 * n_z)
    length, width = grad_out.shape[2:]
    n_modes = SLOTS * n_lat // NB
    inv, m_inv, fwd, m_fwd = lon_consts(n_modes, length, half_z)
    dft, pick, split = lat_consts(rows, n_z)
    operands = [
        grad_out.reshape(length, width), jnp.asarray(inv), jnp.asarray(m_inv), assignment.reshape(1, rows),
        mode_counts.reshape(1, rows), spec_saved.reshape(rows, 2, SLOTS * BS), jnp.asarray(split),
        w1.reshape(2, BS, width), b1.reshape(2, width), w2.reshape(2, BS, width), jnp.asarray(pick),
        jnp.asarray(dft), jnp.asarray(fwd), jnp.asarray(m_fwd),
    ]
    vmem = pltpu.VMEM
    tile = (SLOTS, 2, LANES)
    big = 2 * LANES
    scratch = [vmem(v.shape, v.dtype) for v in operands] + [
        vmem((NB, 2, half_z, 2) + tile, BF16),
        vmem((rows,) + tile, BF16),
        vmem((rows,) + tile, BF16),
        vmem((half_z, 2, NB, 2) + tile, BF16),
        vmem((length, width), BF16),
        vmem((big, big), BF16),
        vmem((big, big), BF16),
        vmem((SLOTS, 2 * rows, LANES), BF16),
        vmem((SLOTS, 2 * rows, LANES), BF16),
        vmem((SLOTS * rows, big), BF16),
        vmem((SLOTS * rows, big), BF16),
        vmem((SLOTS * rows, big), F32),
        vmem((2 * rows, 2 * rows), BF16),
        vmem((2 * rows, 2 * rows), BF16),
        vmem((2 * n_z, 4, jc, LANES), BF16),
        vmem((NB * half_z, 4, jc, LANES), BF16),
    ]
    dma = pltpu.SemaphoreType.DMA
    sems = [
        dma((14,)), dma(()), dma(()), dma(()), dma(()), dma(()), dma(()), dma((SLOTS,)), dma((SLOTS,)),
        dma(()), dma(()),
    ]
    hbm = pl.BlockSpec(memory_space=pl.ANY)
    whole = pl.BlockSpec(memory_space=pltpu.VMEM)
    held = pl.pallas_call(
        functools.partial(kernel, n_sec, n_z),
        out_shape=(
            vmem((length, width), BF16),
            vmem((2, jc, BS), F32),
            vmem((2, jc, BS), F32),
            vmem((2, jc), F32),
        ),
        in_specs=[hbm] * 14,
        out_specs=(whole,) * 4,
        scratch_shapes=scratch + sems,
        compiler_params=pltpu.CompilerParams(collective_id=0, has_side_effects=True),
        name="filter_backward",
    )(*operands)
    gi, gw1, gw2, gb1 = pl.pallas_call(
        store,
        out_shape=tuple(jax.ShapeDtypeStruct(v.shape, v.dtype) for v in held),
        in_specs=[hbm] * 4,
        out_specs=(hbm,) * 4,
        scratch_shapes=[dma((4,))],
        name="store",
    )(*[pltpu.with_memory_space_constraint(v, pltpu.VMEM) for v in held])
    return gi[None, None], jnp.swapaxes(gw1, 1, 2)[None], jnp.swapaxes(gw2, 1, 2)[None], gb1[None]


def solution(mesh):
    return jax.shard_map(
        functools.partial(per_device, mesh.shape["section"], mesh.shape["lat"]),
        mesh=mesh,
        in_specs=(
            P("section", "lat", None, None),
            P("section", None, None, "lat"),
            P("section", None, None, None),
            P("section", None, None, None),
            P("section", None, None),
            P(),
            P(),
        ),
        out_specs=(
            P("section", "lat", None, None),
            P("section", None, None, "lat"),
            P("section", None, None, "lat"),
            P("section", None, "lat"),
        ),
        check_vma=False,
    )
```
